128 devices in a mesh: row: 8 (over z, core), col: 16 (over y, x).
Axes of the slice: x: 4, y: 4, z: 4, core: 2. Of those that a mesh axis runs over, the one named last changes fastest.
Arguments:
- parent_cov: bfloat16 [32768, 32768], P(('row', 'col')), may hold values from -6 to 6
- anc_index: int32 [16384], replicated, may hold values from 0 to 32767, as said below
- fac_rows: bfloat16 [16384, 2048], P('col'), may hold values from -0.125 to 0.125
- inv_factor: bfloat16 [2048, 2048], P(None, 'row'), may hold values from -0.125 to 0.125
- own_inverse: float32 [2048, 2048], P('row', 'col'), may hold values from -6 to 6
Outputs:
- cov_sa: float32 [2048, 16384], P('row', 'col')
- cov_ss: float32 [2048, 2048], P('row', 'col')
The draws below stay inside these ranges and needn't reach their ends.
Inputs may be any that keep to these rules, and one draw needn't show every extreme that they name: `anc_index`: all values are distinct. Split the list into aligned blocks of 2048 entries and the values into ranges of 256 (one device's rows of parent_cov): no block holds more than 32 values of one range, and every block holds exactly 32 values of some range.
All inputs are finite; a program needn't handle non-finite values.
Results may differ from the reference program's by a relative error of at most 0.0049.
Values may be sent and summed in bfloat16 or wider, within the bound.
No kernel may reach another device: no remote copies, remote signals or barrier semaphores. Data moves between devices by JAX's collectives and lax.ppermute only.
A program may use at most 192 MiB of HBM per device.

```python
import jax
import jax.numpy as jnp

NA = 16384
NS = 2048
NP = 32768
PROWS = 256
BLOCK = 2048
MOST = 32


def draw_anc_index(key, part):
    owners = NP // PROWS
    blocks = NA // BLOCK
    half_cap = MOST // 2
    key_amount, key_order, key_local, key_shuffle = jax.random.split(key, 4)
    amounts = jax.random.randint(key_amount, (blocks, owners // 2), 0, half_cap + 1)
    amounts = amounts.at[:, 0].set(half_cap)
    pattern = jnp.stack([amounts, -amounts], axis=-1).reshape(blocks, owners)
    orders = jax.vmap(lambda sub: jax.random.permutation(sub, owners))(jax.random.split(key_order, blocks))
    counts = half_cap + jnp.take_along_axis(pattern, orders, axis=1)
    offsets = jnp.cumsum(counts, axis=0) - counts
    local_perm = jax.vmap(lambda sub: jax.random.permutation(sub, PROWS))(jax.random.split(key_local, owners))
    shuffle_keys = jax.random.split(key_shuffle, blocks)

    def one_block(block_counts, block_offsets, shuffle_key):
        ends = jnp.cumsum(block_counts)
        starts = ends - block_counts
        positions = jnp.arange(BLOCK, dtype=jnp.int32)
        owner_ids = jnp.searchsorted(ends, positions, side='right').astype(jnp.int32)
        slot_rank = positions - starts[owner_ids]
        local_rows = local_perm[owner_ids, block_offsets[owner_ids] + slot_rank]
        values = owner_ids * PROWS + local_rows
        mixing = jax.random.permutation(shuffle_key, BLOCK)
        return values[mixing]
    result = jax.vmap(one_block)(counts, offsets, shuffle_keys)
    return result.reshape(NA).astype(jnp.int32)


def block_scale(own_key, shape, pieces, low, top_value):
    def one(position, parts):
        steps = jax.random.uniform(jax.random.fold_in(jax.random.fold_in(own_key, 6), position), (parts,), jnp.float32, low / len(pieces), top_value / len(pieces))
        return jnp.repeat(jnp.exp(steps), shape[position] // parts).reshape((-1,) + (1,) * (len(shape) - position - 1))

    gain = one(*pieces[0])
    for cut in pieces[1:]:
        gain = gain * one(*cut)
    return gain


def bell_draw(own_key, dims, width, limit, cuts=(), kind=jnp.bfloat16):
    array = jax.random.normal(own_key, dims, jnp.float32) * width
    if len(cuts) > 0:
        array = block_scale(own_key, dims, cuts, -0.22, 0.18) * array
    return jnp.clip(array, min=-limit, max=limit).astype(kind)


def setup_inputs(seed: int = 0) -> dict:
    splits = jax.random.split(jax.random.key(seed), 6)
    parent_cov = bell_draw(splits[0], (NP, NP), 1.0, 6.0, ((0, 128),))
    anc_index = draw_anc_index(jax.random.fold_in(splits[5], 71), 0)
    fac_rows = bell_draw(splits[2], (NA, NS), NS ** -0.5, 0.125, ((0, 16),))
    inv_factor = bell_draw(splits[3], (NS, NS), NS ** -0.5, 0.125, ((1, 8),))
    own_inverse = bell_draw(splits[4], (NS, NS), 1.0, 6.0, ((0, 8), (1, 16)), jnp.float32)
    return {"parent_cov": parent_cov, "anc_index": anc_index, "fac_rows": fac_rows, "inv_factor": inv_factor, "own_inverse": own_inverse}


def reference(parent_cov, anc_index, fac_rows, inv_factor, own_inverse):
    picked = jnp.take(parent_cov, anc_index, axis=0)
    cov_aa = jnp.take(picked, anc_index, axis=1)
    sep_order = inv_factor.shape[0]
    row_ids = jnp.arange(sep_order, dtype=jnp.int32)[:, None]
    col_ids = jnp.arange(sep_order, dtype=jnp.int32)[None, :]
    lower = jnp.where(row_ids >= col_ids, inv_factor, jnp.zeros((), inv_factor.dtype))
    factor_u = jnp.dot(fac_rows, lower, preferred_element_type=jnp.float32).astype(jnp.bfloat16)
    cov_sa = -jnp.dot(factor_u.T, cov_aa, preferred_element_type=jnp.float32)
    sa_rounded = cov_sa.astype(jnp.bfloat16)
    cov_ss = own_inverse - jnp.dot(sa_rounded, factor_u, preferred_element_type=jnp.float32)
    return cov_sa, cov_ss
```

```python
import functools

import jax
import jax.numpy as jnp
from jax import lax
from jax.experimental import pallas as pl
from jax.experimental.pallas import tpu as pltpu
from jax.sharding import PartitionSpec as P

BF = jnp.bfloat16
F32 = jnp.float32
SLOT = 32
LANES = 128
REACH = 10
WIN = 256


def dot_nt(a, b):
    return lax.dot_general(a, b, (((1,), (1,)), ((), ())), preferred_element_type=F32)


def one_hot(targets, base):
    ids = lax.broadcasted_iota(jnp.int32, (WIN, targets.shape[-1]), 0) + base
    return jnp.where(ids == targets, 1.0, 0.0).astype(BF)


def window_rows(table, data, lead, first, base):
    lines = [table[lead + (pl.ds(first + i, 1), slice(None))] for i in range(REACH)]
    hot = jnp.concatenate([one_hot(line, base) for line in lines], axis=1)
    start = pl.multiple_of(first * LANES, LANES)
    rows = data[lead + (pl.ds(start, REACH * LANES), slice(None))]
    return jnp.dot(hot, rows, preferred_element_type=F32)


def select_kernel(ranges, first_ref, count_ref, slots_ref, own_ref, table_ref, cov_ref, out_ref, held):
    step = pl.program_id(0)
    cols = slots_ref.shape[-1]
    blocks = held.shape[0]
    per_step = cov_ref.shape[1] // cols
    fill_steps = ranges // per_step

    @pl.when(step == 0)
    def _():
        extra = held.shape[1] - ranges * SLOT
        held[:, pl.ds(ranges * SLOT, extra), :] = jnp.zeros((blocks, extra, held.shape[2]), BF)

    @pl.when(step < fill_steps)
    def _():
        for k in range(per_step):
            hot = one_hot(slots_ref[k], 0)
            part = dot_nt(hot, cov_ref[:, k * cols:(k + 1) * cols]).astype(BF)
            at = pl.multiple_of((step * per_step + k) * SLOT, SLOT)
            for b in range(blocks):
                held[b, pl.ds(at, SLOT), :] = part[b * SLOT:(b + 1) * SLOT]

    @pl.when(step >= fill_steps)
    def _():
        tile = step - fill_steps
        block = tile // 2
        half = tile % 2
        windows = out_ref.shape[-1] // WIN
        rows_hot = one_hot(own_ref[0], 0)
        for w in range(windows):
            base = (half * windows + w) * WIN
            first = first_ref[tile, w]
            acc = window_rows(table_ref, held, (block,), first, base)

            def more(i, acc):
                return acc + window_rows(table_ref, held, (block,), first + i * REACH, base)

            acc = lax.fori_loop(1, count_ref[tile, w], more, acc)
            out = dot_nt(rows_hot, acc.astype(BF)).astype(BF)
            for b in range(blocks):
                out_ref[b, 0, :, w * WIN:(w + 1) * WIN] = out[b * SLOT:(b + 1) * SLOT]


def select(cov, slots, own, table, firsts, counts, tile_cols):
    rows, width = cov.shape
    ranges, _, cols = slots.shape
    blocks = table.shape[0]
    tiles = firsts.shape[0]
    per_step = 8
    fill = ranges // per_step
    grid_spec = pltpu.PrefetchScalarGridSpec(
        num_scalar_prefetch=2,
        grid=(fill + tiles,),
        in_specs=[
            pl.BlockSpec((per_step, 1, cols), lambda i, f, n: (jnp.minimum(i, fill - 1), 0, 0)),
            pl.BlockSpec((1, 1, cols), lambda i, f, n: (0, 0, 0)),
            pl.BlockSpec(table.shape, lambda i, f, n: (0, 0, 0)),
            pl.BlockSpec((rows, per_step * cols), lambda i, f, n: (0, jnp.minimum(i, fill - 1))),
        ],
        out_specs=pl.BlockSpec(
            (blocks, 1, SLOT, tile_cols), lambda i, f, n: (0, jnp.maximum(i - fill, 0), 0, 0)
        ),
        scratch_shapes=[pltpu.VMEM((blocks, ranges * SLOT + REACH * LANES, rows), BF)],
    )
    return pl.pallas_call(
        functools.partial(select_kernel, ranges),
        grid_spec=grid_spec,
        out_shape=jax.ShapeDtypeStruct((blocks, tiles, SLOT, tile_cols), BF),
        name="select_columns",
    )(firsts, counts, slots, own, table, cov)


def squeeze_kernel(first_ref, count_ref, table_ref, got_ref, out_ref, held, sem):
    rows = got_ref.shape[0]
    copy = pltpu.make_async_copy(got_ref, held.at[pl.ds(0, rows)], sem)
    copy.start()
    extra = held.shape[0] - rows
    held[pl.ds(rows, extra), :] = jnp.zeros((extra, held.shape[1]), BF)
    copy.wait()
    for w in range(out_ref.shape[0] // WIN):
        first = first_ref[w]
        acc = window_rows(table_ref, held, (), first, w * WIN)

        def more(i, acc, first=first, w=w):
            return acc + window_rows(table_ref, held, (), first + i * REACH, w * WIN)

        acc = lax.fori_loop(1, count_ref[w], more, acc)
        out_ref[w * WIN:(w + 1) * WIN, :] = acc.astype(BF)


def squeeze(received, table, firsts, counts, block_len):
    rows, cols = received.shape
    return pl.pallas_call(
        squeeze_kernel,
        in_specs=[
            pl.BlockSpec(memory_space=pltpu.SMEM),
            pl.BlockSpec(memory_space=pltpu.SMEM),
            pl.BlockSpec(memory_space=pltpu.VMEM),
            pl.BlockSpec(memory_space=pl.ANY),
        ],
        out_specs=pl.BlockSpec(memory_space=pltpu.VMEM),
        out_shape=jax.ShapeDtypeStruct((block_len, cols), BF),
        scratch_shapes=[pltpu.VMEM((rows + REACH * LANES, cols), BF), pltpu.SemaphoreType.DMA],
        name="squeeze_rows",
    )(firsts, counts, table, received)


def local(parent_cov, anc_index, fac_rows, inv_factor, own_inverse):
    row_count = lax.axis_size("row")
    col_count = lax.axis_size("col")
    owners = row_count * col_count
    parent_rows = parent_cov.shape[0]
    ancestors = anc_index.shape[0]
    block_len = ancestors // row_count
    tile_cols = ancestors // col_count
    row_index = lax.axis_index("row")
    col_index = lax.axis_index("col")
    device = row_index * col_count + col_index
    i32 = jnp.int32

    own_ids = lax.dynamic_slice_in_dim(anc_index, col_index * tile_cols, tile_cols)
    rank = jnp.sum((own_ids[None, :] < own_ids[:, None]).astype(i32), axis=1)
    perm = (jnp.arange(tile_cols, dtype=i32)[:, None] == rank[None, :]).astype(BF)
    sep_cols = inv_factor.shape[1]
    row_ids = jnp.arange(inv_factor.shape[0], dtype=i32)[:, None]
    col_ids = row_index * sep_cols + jnp.arange(sep_cols, dtype=i32)[None, :]
    lower = jnp.where(row_ids >= col_ids, inv_factor, jnp.zeros((), inv_factor.dtype))
    u_tile = jnp.dot(fac_rows, lower, preferred_element_type=F32).astype(BF)
    u_sorted = jnp.dot(perm, u_tile, preferred_element_type=F32).astype(BF)
    u_cols = lax.all_gather(u_sorted, "row", axis=1, tiled=True)
    share = tile_cols // row_count
    piece = lax.dynamic_slice_in_dim(u_cols, row_index * share, share, axis=0)
    moves = []
    for r in range(row_count):
        for c in range(col_count):
            target = (c // 2) * col_count + (c % 2) * row_count + r
            moves.append((r * col_count + c, target))
    piece = lax.ppermute(piece, ("row", "col"), moves)
    u_block = lax.all_gather(piece, "col", axis=0, tiled=True)

    owner_ids = anc_index // parent_rows
    inner_ids = anc_index % parent_rows
    tile_ids = (jnp.arange(ancestors, dtype=i32) // tile_cols + 1).astype(F32)
    owner_hot = jnp.where(
        owner_ids[None, :] == jnp.arange(owners, dtype=i32)[:, None], tile_ids[None, :], 0.0
    ).astype(BF)
    inner_hot = (inner_ids[:, None] == jnp.arange(parent_rows, dtype=i32)[None, :]).astype(BF)
    tile_of = jnp.dot(owner_hot, inner_hot, preferred_element_type=F32)
    masks = tile_of[None] == jnp.arange(1, col_count + 1, dtype=i32).astype(F32)[:, None, None]
    before = (
        jnp.arange(parent_rows, dtype=i32)[:, None] < jnp.arange(parent_rows, dtype=i32)[None, :]
    ).astype(BF)
    ahead = jnp.dot(
        masks.astype(BF).reshape(col_count * owners, parent_rows), before, preferred_element_type=F32
    ).reshape(col_count, owners, parent_rows)
    number = jnp.sum(masks.astype(F32), axis=2)
    tile_range = jnp.arange(col_count, dtype=i32)
    shifted = jnp.concatenate([jnp.zeros((1, owners), F32), number[:-1]], axis=0)
    base = (tile_range // 2 * SLOT).astype(F32)[:, None] + jnp.where(
        tile_range[:, None] % 2 == 1, shifted, 0.0
    )
    slots = jnp.sum(jnp.where(masks, ahead + base[:, :, None] + 1.0, 0.0), axis=0) - 1.0
    slots = slots.astype(i32).reshape(owners, 1, parent_rows)
    own_slots = lax.dynamic_slice_in_dim(slots, device, 1, axis=0)

    earlier = (
        jnp.arange(owners, dtype=i32)[:, None] < jnp.arange(owners, dtype=i32)[None, :]
    ).astype(BF)
    starts = jnp.dot(number.astype(BF), earlier, preferred_element_type=F32).astype(i32)
    number = number.astype(i32)
    s = jnp.arange(SLOT, dtype=i32)[None, None, :]
    n0, n1 = number[0::2, :, None], number[1::2, :, None]
    p0, p1 = starts[0::2, :, None], starts[1::2, :, None]
    table = jnp.where(s < n0, p0 + s, jnp.where(s < n0 + n1, tile_cols + p1 + s - n0, -1))
    table = table.reshape(row_count, owners * SLOT // LANES, LANES)
    table = jnp.pad(table, ((0, 0), (0, 16), (0, 0)), constant_values=-1)
    per_line = LANES // SLOT
    edges = jnp.arange(tile_cols // WIN, dtype=i32)[None, :, None] * WIN
    lead = jnp.sum((starts + number)[:, None, :] <= edges, axis=2, dtype=i32)
    last = jnp.sum(starts[:, None, :] < edges + WIN, axis=2, dtype=i32) - 1
    firsts = lead // per_line
    counts = (last // per_line - firsts) // REACH + 1

    outgoing = select(parent_cov, slots, own_slots, table, firsts, counts, tile_cols)
    flat_out = outgoing.reshape(owners * SLOT, tile_cols)
    received = lax.all_to_all(flat_out, ("row", "col"), split_axis=0, concat_axis=0, tiled=True)
    own_table = lax.dynamic_slice_in_dim(table, row_index, 1, axis=0)[0]
    own_firsts = lax.dynamic_slice_in_dim(firsts, row_index * 2, 2, axis=0).reshape(-1)
    own_counts = lax.dynamic_slice_in_dim(counts, row_index * 2, 2, axis=0).reshape(-1)
    cov_tile = squeeze(received, own_table, own_firsts, own_counts, block_len)

    part = lax.dot_general(
        u_block, cov_tile, (((0,), (0,)), ((), ())), preferred_element_type=F32
    )
    sa_sorted = lax.psum_scatter(
        (-part).astype(BF), "row", scatter_dimension=0, tiled=True
    ).astype(F32)
    sa_high = sa_sorted.astype(BF)
    ss_part = lax.dot_general(
        u_cols, sa_high, (((0,), (1,)), ((), ())), preferred_element_type=F32
    ).astype(BF)
    ss_all = lax.all_to_all(ss_part, "col", split_axis=0, concat_axis=0, tiled=True)
    sa_low = (sa_sorted - sa_high.astype(F32)).astype(BF)
    cov_sa = jnp.dot(sa_high, perm, preferred_element_type=F32) + jnp.dot(
        sa_low, perm, preferred_element_type=F32
    )
    ss_sum = jnp.sum(ss_all.reshape(col_count, -1, ss_all.shape[1]).astype(F32), axis=0)
    cov_ss = own_inverse - ss_sum.T
    return (cov_sa, cov_ss)


def solution(mesh):
    return jax.shard_map(
        local,
        mesh=mesh,
        in_specs=(P(("row", "col"), None), P(), P("col", None), P(None, "row"), P("row", "col")),
        out_specs=(P("row", "col"), P("row", "col")),
        check_vma=False,
    )
```

```python
import functools

import jax
import jax.numpy as jnp
from jax import lax
from jax.experimental import pallas as pl
from jax.experimental.pallas import tpu as pltpu
from jax.sharding import PartitionSpec as P

BF = jnp.bfloat16
F32 = jnp.float32
I32 = jnp.int32
SLOT = 32
LANES = 128
REACH = 10
LINES = 32
WIN = 256

def dot_nt(a, b):
    return lax.dot_general(a, b, (((1,), (1,)), ((), ())), preferred_element_type=F32)


def dot(a, b):
    return jnp.dot(a, b, preferred_element_type=F32)


def iota(shape, axis):
    return lax.broadcasted_iota(I32, shape, axis)


def ones_where(cond):
    return jnp.where(cond, 1.0, 0.0).astype(BF)


def index_kernel(tiles, anc_ref, slots_ref, table_ref, first_ref, count_ref):
    owners, rows = slots_ref.shape
    chunk = anc_ref.shape[1]
    tile_of = jnp.zeros((owners, rows), F32)
    for j in range(anc_ref.shape[0]):
        ids = anc_ref[j:j + 1, :]
        owner, inner = ids // rows, ids % rows
        tile = ((iota((1, chunk), 1) + j * chunk) // (anc_ref.shape[0] * chunk // tiles) + 1).astype(F32)
        owner_hot = jnp.where(iota((owners, chunk), 0) == owner, tile, 0.0).astype(BF)
        inner_hot = ones_where(iota((rows, chunk), 0) == inner)
        tile_of = tile_of + dot_nt(owner_hot, inner_hot)
    at = iota((rows, rows + LANES), 1)
    before = ones_where((iota((rows, rows + LANES), 0) < at) | (at >= rows))
    below = ones_where(iota((owners, owners), 1) < iota((owners, owners), 0))
    per_line = LANES // SLOT
    lines = owners // per_line
    pick = ones_where(iota((lines, owners), 1) // per_line == iota((lines, owners), 0))
    spread = iota((owners, LANES), 0) % per_line == iota((owners, LANES), 1) // SLOT
    s = (iota((lines, LANES), 1) % SLOT).astype(F32)
    edge = (iota((owners, LANES), 1) * WIN).astype(F32)
    expand = lambda v: dot(pick, jnp.where(spread, v, 0.0).astype(BF))
    slots = jnp.zeros((owners, rows), F32) - 1.0
    tile_len = float(anc_ref.shape[0] * chunk // tiles)
    prev = None
    for c in range(tiles):
        mask = tile_of == float(c + 1)
        both = dot(ones_where(mask), before)
        ahead, number = both[:, :rows], both[:, rows:]
        start = dot(below, number.astype(BF))
        base = float(c // 2 * SLOT + 1)
        lift = ahead + base
        if c % 2:
            lift = lift + jnp.concatenate([prev[0]] * (rows // LANES), axis=1)
        slots = slots + jnp.where(mask, lift, 0.0)
        high = jnp.floor(start * (1.0 / 32.0))
        n = expand(number)
        p = expand(high) * 32.0 + expand(start - high * 32.0)
        end = start + number
        lead = jnp.sum(jnp.where(end <= edge, 1.0, 0.0), axis=0, keepdims=True).astype(I32)
        last = jnp.sum(jnp.where(start < edge + float(WIN), 1.0, 0.0), axis=0, keepdims=True).astype(I32) - 1
        first = lead // per_line
        first_ref[c:c + 1, :] = first
        count_ref[c:c + 1, :] = (last // per_line - first) // REACH + 1
        if c % 2:
            n0, p0 = prev[1], prev[2]
            to = jnp.where(s < n0, p0 + s, jnp.where(s < n0 + n, tile_len + p + s - n0, -1.0))
            table_ref[c // 2, 0:lines, :] = to.astype(I32)
        prev = (number, n, p)
    slots_ref[...] = slots.astype(I32)


def index_tables(anc, owners, rows, tiles):
    lines = owners * SLOT // LANES
    return pl.pallas_call(
        functools.partial(index_kernel, tiles),
        out_shape=(
            jax.ShapeDtypeStruct((owners, rows), I32),
            jax.ShapeDtypeStruct((tiles // 2, lines, LANES), I32),
            jax.ShapeDtypeStruct((tiles, LANES), I32),
            jax.ShapeDtypeStruct((tiles, LANES), I32),
        ),
        cost_estimate=pl.CostEstimate(flops=8 << 30, bytes_accessed=1 << 20, transcendentals=0),
        name="index_tables",
    )(anc.reshape(-1, 2048))


def one_hot(targets, base):
    ids = iota((WIN, targets.shape[-1]), 0) + base
    return ones_where(ids == targets)


def window_hot(table, lead, first, base):
    start = jnp.minimum(first, LINES - REACH)
    lines = []
    for i in range(REACH):
        line = table[lead + (pl.ds(start + i, 1), slice(None))]
        lines.append(one_hot(jnp.where(start + i < first, -1, line), base))
    return start, jnp.concatenate(lines, axis=1)


def sort_kernel(per_step, slots_ref, cov_ref, out_ref):
    cols = slots_ref.shape[-1]
    for k in range(per_step):
        hot = one_hot(slots_ref[pl.ds(pl.program_id(0) * per_step + k, 1), :], 0)
        part = dot_nt(hot, cov_ref[:, k * cols:(k + 1) * cols]).astype(BF)
        for b in range(out_ref.shape[0]):
            out_ref[b, k * SLOT:(k + 1) * SLOT, :] = part[b * SLOT:(b + 1) * SLOT]


def sort_columns(cov, slots, blocks, per_step=16):
    rows, width = cov.shape
    ranges, cols = slots.shape
    return pl.pallas_call(
        functools.partial(sort_kernel, per_step),
        grid=(ranges // per_step,),
        in_specs=[
            pl.BlockSpec(slots.shape, lambda i: (0, 0)),
            pl.BlockSpec((rows, per_step * cols), lambda i: (0, i)),
        ],
        out_specs=pl.BlockSpec((blocks, per_step * SLOT, rows), lambda i: (0, i, 0)),
        out_shape=jax.ShapeDtypeStruct((blocks, ranges * SLOT, rows), BF),
        cost_estimate=pl.CostEstimate(flops=12 << 30, bytes_accessed=32 << 20, transcendentals=0),
        name="sort_columns",
    )(slots, cov)


def pack_kernel(first_ref, count_ref, dev_ref, slots_ref, table_ref, data_ref, out_ref, acc):
    block = pl.program_id(0)
    blocks, group, _, width = out_ref.shape
    windows = width // WIN
    rows_hot = one_hot(slots_ref[pl.ds(dev_ref[0], 1), :], 0)

    def part(first, base):
        start, hot = window_hot(table_ref, (block,), first, base)
        at = pl.multiple_of(start * LANES, LANES)
        return dot(hot, data_ref[0, pl.ds(at, REACH * LANES), :]).astype(BF)

    for job in range(group * windows):
        tile = block * group + job // windows
        acc[job * WIN:(job + 1) * WIN, :] = part(first_ref[tile, job % windows], job * WIN)

    def extra(job, carry):
        tile, w = block * group + job // windows, lax.rem(job, windows)
        at = pl.multiple_of(job * WIN, WIN)

        def more(i, carry):
            acc[pl.ds(at, WIN), :] += part(first_ref[tile, w] + i * REACH, at)
            return carry

        return lax.fori_loop(1, count_ref[tile, w], more, carry)

    lax.fori_loop(0, group * windows, extra, 0)
    for g in range(group):
        out = dot_nt(rows_hot, acc[g * width:(g + 1) * width, :]).astype(BF)
        for b in range(blocks):
            out_ref[b, g] = out[b * SLOT:(b + 1) * SLOT]


def pack_columns(data, slots, table, firsts, counts, device, tile_cols):
    blocks, length, rows = data.shape
    tiles = firsts.shape[0]
    group = tiles // blocks
    grid_spec = pltpu.PrefetchScalarGridSpec(
        num_scalar_prefetch=3,
        grid=(blocks,),
        in_specs=[
            pl.BlockSpec(slots.shape, lambda i, f, n, d: (0, 0)),
            pl.BlockSpec(table.shape, lambda i, f, n, d: (0, 0, 0)),
            pl.BlockSpec((1, length, rows), lambda i, f, n, d: (i, 0, 0)),
        ],
        out_specs=pl.BlockSpec((blocks, group, SLOT, tile_cols), lambda i, f, n, d: (0, i, 0, 0)),
        scratch_shapes=[pltpu.VMEM((group * tile_cols, rows), BF)],
    )
    return pl.pallas_call(
        pack_kernel,
        grid_spec=grid_spec,
        out_shape=jax.ShapeDtypeStruct((blocks, tiles, SLOT, tile_cols), BF),
        cost_estimate=pl.CostEstimate(flops=12 << 30, bytes_accessed=24 << 20, transcendentals=0),
        name="pack_columns",
    )(firsts, counts, device, slots, table, data)


def load_lhs(z, u_ref, lhs, sems):
    rows, cols = u_ref.shape[1:]
    return [
        pltpu.make_async_copy(
            u_ref.at[4 * z + 2 * half + core],
            lhs.at[pl.ds(core * rows, rows), pl.ds(half * cols, cols)],
            sems.at[2 * half + core],
        )
        for half in range(2) for core in range(2)
    ]


def start_loads(steps, pos_ref, u_ref, lhs, sems):
    jobs = []
    for n, step in enumerate(steps):
        jobs.append(load_lhs(lax.rem(pos_ref[0] + step, 4), u_ref, lhs.at[n], sems.at[n]))
        for copy in jobs[n]:
            copy.start()
    return jobs


def multiply(jobs, lhs, tile_ref, core, keep_ref, give_ref):
    half = keep_ref.shape[2]
    give = pl.multiple_of((1 - core) * half, half)
    keep = pl.multiple_of(core * half, half)
    for n, copies in enumerate(jobs):
        for copy in copies:
            copy.wait()
        give_ref[n] = dot(lhs[n], tile_ref[:, pl.ds(give, half)])
        keep_ref[n] = dot(lhs[n], tile_ref[:, pl.ds(keep, half)])


def first_kernel(steps, pos_ref, first_ref, count_ref, table_ref, got_ref, u_ref,
                 tile_ref, keep_ref, give_ref, held, lhs, got_sem, lhs_sems):
    z, core = pos_ref[0], pos_ref[1]
    load = pltpu.make_async_copy(got_ref, held, got_sem)
    load.start()
    jobs = start_loads(steps, pos_ref, u_ref, lhs, lhs_sems)
    per_line = LANES // SLOT
    span = REACH * per_line
    windows = tile_ref.shape[0] // WIN
    block = 2 * z + core

    def part(first, base):
        start, hot = window_hot(table_ref, (block,), first, base)
        data = held[pl.ds(start * per_line, span)].reshape(REACH * LANES, held.shape[-1])
        return dot(hot, data).astype(BF)

    load.wait()
    for w in range(windows):
        tile, v = 2 * block + w // (windows // 2), w % (windows // 2)
        tile_ref[w * WIN:(w + 1) * WIN, :] = part(first_ref[tile, v], w * WIN)

    def window(w, carry):
        tile, v = 2 * block + w // (windows // 2), lax.rem(w, windows // 2)
        at = pl.multiple_of(w * WIN, WIN)

        def more(i, carry):
            tile_ref[pl.ds(at, WIN), :] += part(first_ref[tile, v] + i * REACH, at)
            return carry

        return lax.fori_loop(1, count_ref[tile, v], more, carry)

    lax.fori_loop(0, windows, window, 0)
    multiply(jobs, lhs, tile_ref, core, keep_ref, give_ref)


def next_kernel(steps, pos_ref, u_ref, tile_ref, keep_ref, give_ref, lhs, sems):
    jobs = start_loads(steps, pos_ref, u_ref, lhs, sems)
    multiply(jobs, lhs, tile_ref, pos_ref[1], keep_ref, give_ref)


def first_shares(steps, position, firsts, counts, table, received, u_block):
    owners, _, cols = received.shape
    rows, depth = 2 * u_block.shape[1], 2 * u_block.shape[2]
    smem = pl.BlockSpec(memory_space=pltpu.SMEM)
    vmem = pl.BlockSpec(memory_space=pltpu.VMEM)
    hbm = pl.BlockSpec(memory_space=pl.ANY)
    share = jax.ShapeDtypeStruct((len(steps), rows, cols // 2), F32)
    return pl.pallas_call(
        functools.partial(first_kernel, steps),
        in_specs=[smem, smem, smem, vmem, hbm, hbm],
        out_specs=(vmem, vmem, vmem),
        out_shape=(jax.ShapeDtypeStruct((depth, cols), BF), share, share),
        scratch_shapes=[
            pltpu.VMEM((owners, SLOT, cols), BF),
            pltpu.VMEM((len(steps), rows, depth), BF),
            pltpu.SemaphoreType.DMA,
            pltpu.SemaphoreType.DMA((len(steps), 4)),
        ],
        cost_estimate=pl.CostEstimate(flops=24 << 30, bytes_accessed=24 << 20, transcendentals=0),
        name="squeeze_and_first_shares",
    )(position, firsts, counts, table, received, u_block)


def next_shares(steps, position, u_block, tile):
    depth, cols = tile.shape
    rows = 2 * u_block.shape[1]
    smem = pl.BlockSpec(memory_space=pltpu.SMEM)
    vmem = pl.BlockSpec(memory_space=pltpu.VMEM)
    hbm = pl.BlockSpec(memory_space=pl.ANY)
    share = jax.ShapeDtypeStruct((len(steps), rows, cols // 2), F32)
    return pl.pallas_call(
        functools.partial(next_kernel, steps),
        in_specs=[smem, hbm, vmem],
        out_specs=(vmem, vmem),
        out_shape=(share, share),
        scratch_shapes=[
            pltpu.VMEM((len(steps), rows, depth), BF),
            pltpu.SemaphoreType.DMA((len(steps), 4)),
        ],
        cost_estimate=pl.CostEstimate(flops=12 << 30, bytes_accessed=16 << 20, transcendentals=0),
        name="next_shares",
    )(position, u_block, tile)


def pairs(target):
    result = []
    for r in range(8):
        for c in range(16):
            z, core, y, x = target(r // 2, r % 2, c // 4, c % 4)
            result.append((r * 16 + c, (2 * z + core) * 16 + 4 * y + x))
    return result


def local(parent_cov, anc_index, fac_rows, inv_factor, own_inverse):
    row_count = lax.axis_size("row")
    col_count = lax.axis_size("col")
    owners = row_count * col_count
    parent_rows = parent_cov.shape[0]
    tile_cols = anc_index.shape[0] // col_count
    sep_cols = inv_factor.shape[1]
    row_index = lax.axis_index("row")
    col_index = lax.axis_index("col")
    core = row_index % 2
    device = jnp.reshape(row_index * col_count + col_index, (1,)).astype(I32)
    position = jnp.stack([row_index // 2, core]).astype(I32)
    both = ("row", "col")
    swap = pairs(lambda z, core, y, x: (z, 1 - core, y, x))

    own_ids = lax.dynamic_slice_in_dim(anc_index, col_index * tile_cols, tile_cols)
    rank = jnp.sum((own_ids[None, :] < own_ids[:, None]).astype(I32), axis=1)
    perm = (jnp.arange(tile_cols, dtype=I32)[:, None] == rank[None, :]).astype(BF)
    row_ids = jnp.arange(inv_factor.shape[0], dtype=I32)[:, None]
    col_ids = row_index * sep_cols + jnp.arange(sep_cols, dtype=I32)[None, :]
    lower = jnp.where(row_ids >= col_ids, inv_factor, jnp.zeros((), inv_factor.dtype))
    u_tile = jnp.dot(fac_rows, lower, preferred_element_type=F32).astype(BF)
    u_t = lax.dot_general(
        u_tile, perm, (((0,), (1,)), ((), ())), preferred_element_type=F32
    ).astype(BF)
    piece = lax.ppermute(
        u_t, both, pairs(lambda z, core, y, x: (y, x // 2, z, 2 * (x % 2) + core))
    )
    slots, table, firsts, counts = index_tables(anc_index, owners, parent_rows, col_count)
    data = sort_columns(parent_cov, slots, row_count)
    piece, data = lax.optimization_barrier((piece, data))
    u_block = lax.all_gather(piece, "col", axis=0)
    outgoing = pack_columns(data, slots, table, firsts, counts, device, tile_cols)
    outgoing, u_t = lax.optimization_barrier((outgoing, u_t))
    u_cols = lax.all_gather(u_t, "row", axis=0, tiled=True)
    flat_out = outgoing.reshape(owners * SLOT, tile_cols)
    received = lax.all_to_all(flat_out, both, split_axis=0, concat_axis=0, tiled=True)
    received = received.reshape(owners, SLOT, tile_cols)

    tile, keep, give = first_shares((2, 1), position, firsts, counts, table, received, u_block)
    first = (keep + lax.ppermute(give, both, swap)).astype(BF)
    keep, give = next_shares((3, 0), position, u_block, tile)
    second = keep + lax.ppermute(give, both, swap)
    total = second[1]
    for step, share in ((2, first[0]), (1, first[1]), (3, second[0].astype(BF))):
        share = lax.ppermute(
            share, both, pairs(lambda z, core, y, x, step=step: ((z + step) % 4, core, y, x))
        )
        total = total + share.astype(F32)
    total = -total
    kept = lax.dynamic_slice_in_dim(total, core * sep_cols, sep_cols, axis=0)
    given = lax.dynamic_slice_in_dim(total, (1 - core) * sep_cols, sep_cols, axis=0)
    taken = lax.ppermute(given, both, swap)
    sa_sorted = jnp.concatenate(
        [jnp.where(core == 0, kept, taken), jnp.where(core == 0, taken, kept)], axis=1
    )

    sa_high = sa_sorted.astype(BF)
    ss_part = dot_nt(u_cols, sa_high).astype(BF)
    ss_all = lax.all_to_all(ss_part, "col", split_axis=0, concat_axis=0, tiled=True)
    sa_low = (sa_sorted - sa_high.astype(F32)).astype(BF)
    cov_sa = dot(sa_high, perm) + dot(sa_low, perm)
    ss_sum = jnp.sum(ss_all.reshape(col_count, -1, ss_all.shape[1]).astype(F32), axis=0)
    cov_ss = own_inverse - ss_sum.T
    return (cov_sa, cov_ss)


def solution(mesh):
    return jax.shard_map(
        local,
        mesh=mesh,
        in_specs=(P(("row", "col"), None), P(), P("col", None), P(None, "row"), P("row", "col")),
        out_specs=(P("row", "col"), P("row", "col")),
        check_vma=False,
    )
```

```python
import functools

import jax
import jax.numpy as jnp
from jax import lax
from jax.experimental import pallas as pl
from jax.experimental.pallas import tpu as pltpu
from jax.sharding import PartitionSpec as P

BF = jnp.bfloat16
F32 = jnp.float32
I32 = jnp.int32
SLOT = 32
LANES = 128
REACH = 10
LINES = 32
WIN = 256

def dot_nt(a, b):
    return lax.dot_general(a, b, (((1,), (1,)), ((), ())), preferred_element_type=F32)


def dot(a, b):
    return jnp.dot(a, b, preferred_element_type=F32)


def iota(shape, axis):
    return lax.broadcasted_iota(I32, shape, axis)


def ones_where(cond):
    return jnp.where(cond, 1.0, 0.0).astype(BF)


def index_kernel(tiles, anc_ref, slots_ref, table_ref, first_ref, count_ref):
    owners, rows = slots_ref.shape
    chunk = anc_ref.shape[1]
    tile_of = jnp.zeros((owners, rows), F32)
    for j in range(anc_ref.shape[0]):
        ids = anc_ref[j:j + 1, :]
        owner, inner = ids // rows, ids % rows
        tile = ((iota((1, chunk), 1) + j * chunk) // (anc_ref.shape[0] * chunk // tiles) + 1).astype(F32)
        owner_hot = jnp.where(iota((owners, chunk), 0) == owner, tile, 0.0).astype(BF)
        inner_hot = ones_where(iota((rows, chunk), 0) == inner)
        tile_of = tile_of + dot_nt(owner_hot, inner_hot)
    at = iota((rows, rows + LANES), 1)
    before = ones_where((iota((rows, rows + LANES), 0) < at) | (at >= rows))
    below = ones_where(iota((owners, owners), 1) < iota((owners, owners), 0))
    per_line = LANES // SLOT
    lines = owners // per_line
    pick = ones_where(iota((lines, owners), 1) // per_line == iota((lines, owners), 0))
    spread = iota((owners, LANES), 0) % per_line == iota((owners, LANES), 1) // SLOT
    s = (iota((lines, LANES), 1) % SLOT).astype(F32)
    edge = (iota((owners, LANES), 1) * WIN).astype(F32)
    expand = lambda v: dot(pick, jnp.where(spread, v, 0.0).astype(BF))
    slots = jnp.zeros((owners, rows), F32) - 1.0
    tile_len = float(anc_ref.shape[0] * chunk // tiles)
    prev = None
    for c in range(tiles):
        mask = tile_of == float(c + 1)
        both = dot(ones_where(mask), before)
        ahead, number = both[:, :rows], both[:, rows:]
        start = dot(below, number.astype(BF))
        base = float(c // 2 * SLOT + 1)
        lift = ahead + base
        if c % 2:
            lift = lift + jnp.concatenate([prev[0]] * (rows // LANES), axis=1)
        slots = slots + jnp.where(mask, lift, 0.0)
        high = jnp.floor(start * (1.0 / 32.0))
        n = expand(number)
        p = expand(high) * 32.0 + expand(start - high * 32.0)
        end = start + number
        lead = jnp.sum(jnp.where(end <= edge, 1.0, 0.0), axis=0, keepdims=True).astype(I32)
        last = jnp.sum(jnp.where(start < edge + float(WIN), 1.0, 0.0), axis=0, keepdims=True).astype(I32) - 1
        first = lead // per_line
        first_ref[c:c + 1, :] = first
        count_ref[c:c + 1, :] = (last // per_line - first) // REACH + 1
        if c % 2:
            n0, p0 = prev[1], prev[2]
            to = jnp.where(s < n0, p0 + s, jnp.where(s < n0 + n, tile_len + p + s - n0, -1.0))
            table_ref[c // 2, 0:lines, :] = to.astype(I32)
        prev = (number, n, p)
    slots_ref[...] = slots.astype(I32)


def index_tables(anc, owners, rows, tiles):
    lines = owners * SLOT // LANES
    return pl.pallas_call(
        functools.partial(index_kernel, tiles),
        out_shape=(
            jax.ShapeDtypeStruct((owners, rows), I32),
            jax.ShapeDtypeStruct((tiles // 2, lines, LANES), I32),
            jax.ShapeDtypeStruct((tiles, LANES), I32),
            jax.ShapeDtypeStruct((tiles, LANES), I32),
        ),
        cost_estimate=pl.CostEstimate(flops=8 << 30, bytes_accessed=1 << 20, transcendentals=0),
        compiler_params=pltpu.CompilerParams(vmem_limit_bytes=24 << 20),
        name="index_tables",
    )(anc.reshape(-1, 2048))


def one_hot(targets, base):
    ids = iota((WIN, targets.shape[-1]), 0) + base
    return ones_where(ids == targets)


def window_hot(table, lead, first, base):
    start = jnp.minimum(first, LINES - REACH)
    lines = []
    for i in range(REACH):
        line = table[lead + (pl.ds(start + i, 1), slice(None))]
        lines.append(one_hot(jnp.where(start + i < first, -1, line), base))
    return start, jnp.concatenate(lines, axis=1)


def sort_kernel(per_step, slots_ref, cov_ref, out_ref):
    cols = slots_ref.shape[-1]
    for k in range(per_step):
        hot = one_hot(slots_ref[pl.ds(pl.program_id(0) * per_step + k, 1), :], 0)
        part = dot_nt(hot, cov_ref[:, k * cols:(k + 1) * cols]).astype(BF)
        at = pl.multiple_of((pl.program_id(0) * per_step + k) * SLOT, SLOT)
        for b in range(out_ref.shape[0]):
            out_ref[b, pl.ds(at, SLOT), :] = part[b * SLOT:(b + 1) * SLOT]


def sort_columns(cov, slots, blocks, per_step=32):
    rows, width = cov.shape
    ranges, cols = slots.shape
    return pl.pallas_call(
        functools.partial(sort_kernel, per_step),
        grid=(ranges // per_step,),
        in_specs=[
            pl.BlockSpec(slots.shape, lambda i: (0, 0)),
            pl.BlockSpec((rows, per_step * cols), lambda i: (0, i)),
        ],
        out_specs=pl.BlockSpec(memory_space=pltpu.VMEM),
        out_shape=pltpu.VMEM((blocks, ranges * SLOT, rows), BF),
        cost_estimate=pl.CostEstimate(flops=12 << 30, bytes_accessed=32 << 20, transcendentals=0),
        compiler_params=pltpu.CompilerParams(vmem_limit_bytes=24 << 20),
        name="sort_columns",
    )(slots, cov)


def pack_kernel(first_ref, count_ref, dev_ref, slots_ref, table_ref, data_ref, out_ref, acc):
    block = pl.program_id(0)
    blocks, group, _, width = out_ref.shape
    windows = width // WIN
    rows_hot = one_hot(slots_ref[pl.ds(dev_ref[0], 1), :], 0)

    def part(first, base):
        start, hot = window_hot(table_ref, (block,), first, base)
        at = pl.multiple_of(start * LANES, LANES)
        return dot(hot, data_ref[block, pl.ds(at, REACH * LANES), :]).astype(BF)

    for job in range(group * windows):
        tile = block * group + job // windows
        acc[job * WIN:(job + 1) * WIN, :] = part(first_ref[tile, job % windows], job * WIN)

    def extra(job, carry):
        tile, w = block * group + job // windows, lax.rem(job, windows)
        at = pl.multiple_of(job * WIN, WIN)

        def more(i, carry):
            acc[pl.ds(at, WIN), :] += part(first_ref[tile, w] + i * REACH, at)
            return carry

        return lax.fori_loop(1, count_ref[tile, w], more, carry)

    most = count_ref[block * group, 0]
    for job in range(1, group * windows):
        most = jnp.maximum(most, count_ref[block * group + job // windows, job % windows])

    @pl.when(most > 1)
    def _():
        lax.fori_loop(0, group * windows, extra, 0)

    for g in range(group):
        out = dot_nt(rows_hot, acc[g * width:(g + 1) * width, :]).astype(BF)
        for b in range(blocks):
            out_ref[b, g] = out[b * SLOT:(b + 1) * SLOT]


def pack_columns(data, slots, table, firsts, counts, device, tile_cols):
    blocks, length, rows = data.shape
    tiles = firsts.shape[0]
    group = tiles // blocks
    grid_spec = pltpu.PrefetchScalarGridSpec(
        num_scalar_prefetch=3,
        grid=(blocks,),
        in_specs=[
            pl.BlockSpec(slots.shape, lambda i, f, n, d: (0, 0)),
            pl.BlockSpec(table.shape, lambda i, f, n, d: (0, 0, 0)),
            pl.BlockSpec(memory_space=pltpu.VMEM),
        ],
        out_specs=pl.BlockSpec((blocks, group, SLOT, tile_cols), lambda i, f, n, d: (0, i, 0, 0)),
        scratch_shapes=[pltpu.VMEM((group * tile_cols, rows), BF)],
    )
    return pl.pallas_call(
        pack_kernel,
        grid_spec=grid_spec,
        out_shape=jax.ShapeDtypeStruct((blocks, tiles, SLOT, tile_cols), BF),
        cost_estimate=pl.CostEstimate(flops=12 << 30, bytes_accessed=24 << 20, transcendentals=0),
        compiler_params=pltpu.CompilerParams(vmem_limit_bytes=24 << 20),
        name="pack_columns",
    )(firsts, counts, device, slots, table, data)


def load_lhs(z, u_ref, lhs, sems):
    rows, cols = u_ref.shape[1:]
    return [
        pltpu.make_async_copy(
            u_ref.at[4 * z + 2 * half + core],
            lhs.at[pl.ds(core * rows, rows), pl.ds(half * cols, cols)],
            sems.at[2 * half + core],
        )
        for half in range(2) for core in range(2)
    ]


def start_loads(steps, pos_ref, u_ref, lhs, sems):
    jobs = []
    for n, step in enumerate(steps):
        jobs.append(load_lhs(lax.rem(pos_ref[0] + step, 4), u_ref, lhs.at[n], sems.at[n]))
        for copy in jobs[n]:
            copy.start()
    return jobs


def multiply(jobs, lhs, tile_ref, core, keep_ref, give_ref):
    half = keep_ref.shape[2]
    give = pl.multiple_of((1 - core) * half, half)
    keep = pl.multiple_of(core * half, half)
    for n, copies in enumerate(jobs):
        for copy in copies:
            copy.wait()
        give_ref[n] = dot(lhs[n], tile_ref[:, pl.ds(give, half)])
        keep_ref[n] = dot(lhs[n], tile_ref[:, pl.ds(keep, half)])


def first_kernel(steps, pos_ref, first_ref, count_ref, table_ref, got_ref, u_ref,
                 tile_ref, keep_ref, give_ref, held, lhs, got_sem, lhs_sems):
    z, core = pos_ref[0], pos_ref[1]
    load = pltpu.make_async_copy(got_ref, held, got_sem)
    load.start()
    jobs = start_loads(steps, pos_ref, u_ref, lhs, lhs_sems)
    per_line = LANES // SLOT
    span = REACH * per_line
    windows = tile_ref.shape[0] // WIN
    block = 2 * z + core

    def part(first, base):
        start, hot = window_hot(table_ref, (block,), first, base)
        data = held[pl.ds(start * per_line, span)].reshape(REACH * LANES, held.shape[-1])
        return dot(hot, data).astype(BF)

    load.wait()
    for w in range(windows):
        tile, v = 2 * block + w // (windows // 2), w % (windows // 2)
        tile_ref[w * WIN:(w + 1) * WIN, :] = part(first_ref[tile, v], w * WIN)

    def window(w, carry):
        tile, v = 2 * block + w // (windows // 2), lax.rem(w, windows // 2)
        at = pl.multiple_of(w * WIN, WIN)

        def more(i, carry):
            tile_ref[pl.ds(at, WIN), :] += part(first_ref[tile, v] + i * REACH, at)
            return carry

        return lax.fori_loop(1, count_ref[tile, v], more, carry)

    lax.fori_loop(0, windows, window, 0)
    multiply(jobs, lhs, tile_ref, core, keep_ref, give_ref)


def next_kernel(steps, pos_ref, u_ref, tile_ref, keep_ref, give_ref, lhs, sems):
    jobs = start_loads(steps, pos_ref, u_ref, lhs, sems)
    multiply(jobs, lhs, tile_ref, pos_ref[1], keep_ref, give_ref)


def first_shares(steps, position, firsts, counts, table, received, u_block):
    owners, _, cols = received.shape
    rows, depth = 2 * u_block.shape[1], 2 * u_block.shape[2]
    smem = pl.BlockSpec(memory_space=pltpu.SMEM)
    vmem = pl.BlockSpec(memory_space=pltpu.VMEM)
    hbm = pl.BlockSpec(memory_space=pl.ANY)
    share = jax.ShapeDtypeStruct((len(steps), rows, cols // 2), F32)
    return pl.pallas_call(
        functools.partial(first_kernel, steps),
        in_specs=[smem, smem, smem, vmem, hbm, hbm],
        out_specs=(vmem, vmem, vmem),
        out_shape=(pltpu.VMEM((depth, cols), BF), share, share),
        scratch_shapes=[
            pltpu.VMEM((owners, SLOT, cols), BF),
            pltpu.VMEM((len(steps), rows, depth), BF),
            pltpu.SemaphoreType.DMA,
            pltpu.SemaphoreType.DMA((len(steps), 4)),
        ],
        cost_estimate=pl.CostEstimate(flops=24 << 30, bytes_accessed=24 << 20, transcendentals=0),
        compiler_params=pltpu.CompilerParams(vmem_limit_bytes=36 << 20),
        name="squeeze_and_first_shares",
    )(position, firsts, counts, table, received, u_block)


def next_shares(steps, position, u_block, tile):
    depth, cols = tile.shape
    rows = 2 * u_block.shape[1]
    smem = pl.BlockSpec(memory_space=pltpu.SMEM)
    vmem = pl.BlockSpec(memory_space=pltpu.VMEM)
    hbm = pl.BlockSpec(memory_space=pl.ANY)
    share = jax.ShapeDtypeStruct((len(steps), rows, cols // 2), F32)
    return pl.pallas_call(
        functools.partial(next_kernel, steps),
        in_specs=[smem, hbm, vmem],
        out_specs=(vmem, vmem),
        out_shape=(share, share),
        scratch_shapes=[
            pltpu.VMEM((len(steps), rows, depth), BF),
            pltpu.SemaphoreType.DMA((len(steps), 4)),
        ],
        cost_estimate=pl.CostEstimate(flops=12 << 30, bytes_accessed=16 << 20, transcendentals=0),
        compiler_params=pltpu.CompilerParams(vmem_limit_bytes=24 << 20),
        name="next_shares",
    )(position, u_block, tile)


def pairs(target):
    result = []
    for r in range(8):
        for c in range(16):
            z, core, y, x = target(r // 2, r % 2, c // 4, c % 4)
            result.append((r * 16 + c, (2 * z + core) * 16 + 4 * y + x))
    return result


def local(parent_cov, anc_index, fac_rows, inv_factor, own_inverse):
    row_count = lax.axis_size("row")
    col_count = lax.axis_size("col")
    owners = row_count * col_count
    parent_rows = parent_cov.shape[0]
    tile_cols = anc_index.shape[0] // col_count
    sep_cols = inv_factor.shape[1]
    row_index = lax.axis_index("row")
    col_index = lax.axis_index("col")
    core = row_index % 2
    device = jnp.reshape(row_index * col_count + col_index, (1,)).astype(I32)
    position = jnp.stack([row_index // 2, core]).astype(I32)
    both = ("row", "col")
    swap = pairs(lambda z, core, y, x: (z, 1 - core, y, x))

    own_ids = lax.dynamic_slice_in_dim(anc_index, col_index * tile_cols, tile_cols)
    rank = jnp.sum((own_ids[None, :] < own_ids[:, None]).astype(I32), axis=1)
    perm = (jnp.arange(tile_cols, dtype=I32)[:, None] == rank[None, :]).astype(BF)
    row_ids = jnp.arange(inv_factor.shape[0], dtype=I32)[:, None]
    col_ids = row_index * sep_cols + jnp.arange(sep_cols, dtype=I32)[None, :]
    lower = jnp.where(row_ids >= col_ids, inv_factor, jnp.zeros((), inv_factor.dtype))
    u_tile = jnp.dot(fac_rows, lower, preferred_element_type=F32).astype(BF)
    u_t = lax.dot_general(
        u_tile, perm, (((0,), (1,)), ((), ())), preferred_element_type=F32
    ).astype(BF)
    piece = lax.ppermute(
        u_t, both, pairs(lambda z, core, y, x: (y, x // 2, z, 2 * (x % 2) + core))
    )
    slots, table, firsts, counts = index_tables(anc_index, owners, parent_rows, col_count)
    data = sort_columns(parent_cov, slots, row_count)
    piece, data = lax.optimization_barrier((piece, data))
    u_block = lax.all_gather(piece, "col", axis=0)
    outgoing = pack_columns(data, slots, table, firsts, counts, device, tile_cols)
    outgoing, u_t = lax.optimization_barrier((outgoing, u_t))
    u_cols = lax.all_gather(u_t, "row", axis=0, tiled=True)
    flat_out = outgoing.reshape(owners * SLOT, tile_cols)
    received = lax.all_to_all(flat_out, both, split_axis=0, concat_axis=0, tiled=True)
    received = received.reshape(owners, SLOT, tile_cols)

    tile, keep, give = first_shares((2, 1), position, firsts, counts, table, received, u_block)
    first = (keep + lax.ppermute(give, both, swap)).astype(BF)
    keep, give = next_shares((3, 0), position, u_block, tile)
    second = keep + lax.ppermute(give, both, swap)
    total = second[1]
    for step, share in ((2, first[0]), (1, first[1]), (3, second[0].astype(BF))):
        share = lax.ppermute(
            share, both, pairs(lambda z, core, y, x, step=step: ((z + step) % 4, core, y, x))
        )
        total = total + share.astype(F32)
    total = -total
    kept = lax.dynamic_slice_in_dim(total, core * sep_cols, sep_cols, axis=0)
    given = lax.dynamic_slice_in_dim(total, (1 - core) * sep_cols, sep_cols, axis=0)
    taken = lax.ppermute(given, both, swap)
    sa_sorted = jnp.concatenate(
        [jnp.where(core == 0, kept, taken), jnp.where(core == 0, taken, kept)], axis=1
    )

    sa_high = sa_sorted.astype(BF)
    ss_part = dot_nt(u_cols, sa_high).astype(BF)
    ss_all = lax.all_to_all(ss_part, "col", split_axis=0, concat_axis=0, tiled=True)
    sa_low = (sa_sorted - sa_high.astype(F32)).astype(BF)
    cov_sa = dot(sa_high, perm) + dot(sa_low, perm)
    ss_sum = jnp.sum(ss_all.reshape(col_count, -1, ss_all.shape[1]).astype(F32), axis=0)
    cov_ss = own_inverse - ss_sum.T
    return (cov_sa, cov_ss)


def solution(mesh):
    return jax.shard_map(
        local,
        mesh=mesh,
        in_specs=(P(("row", "col"), None), P(), P("col", None), P(None, "row"), P("row", "col")),
        out_specs=(P("row", "col"), P("row", "col")),
        check_vma=False,
    )
```

```python
import functools

import jax
import jax.numpy as jnp
from jax import lax
from jax.experimental import pallas as pl
from jax.experimental.pallas import tpu as pltpu
from jax.sharding import PartitionSpec as P

BF = jnp.bfloat16
F32 = jnp.float32
I32 = jnp.int32
SLOT = 32
LANES = 128
REACH = 10
LINES = 32
WIN = 256

def dot_nt(a, b):
    return lax.dot_general(a, b, (((1,), (1,)), ((), ())), preferred_element_type=F32)


def dot(a, b):
    return jnp.dot(a, b, preferred_element_type=F32)


def iota(shape, axis):
    return lax.broadcasted_iota(I32, shape, axis)


def ones_where(cond):
    return jnp.where(cond, 1.0, 0.0).astype(BF)


def index_kernel(tiles, anc_ref, slots_ref, table_ref, first_ref, count_ref):
    owners, rows = slots_ref.shape
    chunk = anc_ref.shape[1]
    tile_of = jnp.zeros((owners, rows), F32)
    for j in range(anc_ref.shape[0]):
        ids = anc_ref[j:j + 1, :]
        owner, inner = ids // rows, ids % rows
        tile = ((iota((1, chunk), 1) + j * chunk) // (anc_ref.shape[0] * chunk // tiles) + 1).astype(F32)
        owner_hot = jnp.where(iota((owners, chunk), 0) == owner, tile, 0.0).astype(BF)
        inner_hot = ones_where(iota((rows, chunk), 0) == inner)
        tile_of = tile_of + dot_nt(owner_hot, inner_hot)
    at = iota((rows, rows + LANES), 1)
    before = ones_where((iota((rows, rows + LANES), 0) < at) | (at >= rows))
    below = ones_where(iota((owners, owners), 1) < iota((owners, owners), 0))
    per_line = LANES // SLOT
    lines = owners // per_line
    pick = ones_where(iota((lines, owners), 1) // per_line == iota((lines, owners), 0))
    spread = iota((owners, LANES), 0) % per_line == iota((owners, LANES), 1) // SLOT
    s = (iota((lines, LANES), 1) % SLOT).astype(F32)
    edge = (iota((owners, LANES), 1) * WIN).astype(F32)
    expand = lambda v: dot(pick, jnp.where(spread, v, 0.0).astype(BF))
    slots = jnp.zeros((owners, rows), F32) - 1.0
    tile_len = float(anc_ref.shape[0] * chunk // tiles)
    prev = None
    for c in range(tiles):
        mask = tile_of == float(c + 1)
        both = dot(ones_where(mask), before)
        ahead, number = both[:, :rows], both[:, rows:]
        start = dot(below, number.astype(BF))
        base = float(c // 2 * SLOT + 1)
        lift = ahead + base
        if c % 2:
            lift = lift + jnp.concatenate([prev[0]] * (rows // LANES), axis=1)
        slots = slots + jnp.where(mask, lift, 0.0)
        high = jnp.floor(start * (1.0 / 32.0))
        n = expand(number)
        p = expand(high) * 32.0 + expand(start - high * 32.0)
        end = start + number
        lead = jnp.sum(jnp.where(end <= edge, 1.0, 0.0), axis=0, keepdims=True).astype(I32)
        last = jnp.sum(jnp.where(start < edge + float(WIN), 1.0, 0.0), axis=0, keepdims=True).astype(I32) - 1
        first = lead // per_line
        first_ref[c:c + 1, :] = first
        count_ref[c:c + 1, :] = (last // per_line - first) // REACH + 1
        if c % 2:
            n0, p0 = prev[1], prev[2]
            to = jnp.where(s < n0, p0 + s, jnp.where(s < n0 + n, tile_len + p + s - n0, -1.0))
            table_ref[c // 2, 0:lines, :] = to.astype(I32)
        prev = (number, n, p)
    slots_ref[...] = slots.astype(I32)


def index_tables(anc, owners, rows, tiles):
    lines = owners * SLOT // LANES
    return pl.pallas_call(
        functools.partial(index_kernel, tiles),
        out_shape=(
            jax.ShapeDtypeStruct((owners, rows), I32),
            jax.ShapeDtypeStruct((tiles // 2, lines, LANES), I32),
            jax.ShapeDtypeStruct((tiles, LANES), I32),
            jax.ShapeDtypeStruct((tiles, LANES), I32),
        ),
        cost_estimate=pl.CostEstimate(flops=8 << 30, bytes_accessed=1 << 20, transcendentals=0),
        name="index_tables",
    )(anc.reshape(-1, 2048))


def one_hot(targets, base):
    ids = iota((WIN, targets.shape[-1]), 0) + base
    return ones_where(ids == targets)


def window_hot(table, lead, first, base):
    start = jnp.minimum(first, LINES - REACH)
    lines = []
    for i in range(REACH):
        line = table[lead + (pl.ds(start + i, 1), slice(None))]
        lines.append(one_hot(jnp.where(start + i < first, -1, line), base))
    return start, jnp.concatenate(lines, axis=1)


def sort_kernel(per_step, slots_ref, cov_ref, out_ref):
    cols = slots_ref.shape[-1]
    for k in range(per_step):
        hot = one_hot(slots_ref[pl.ds(pl.program_id(0) * per_step + k, 1), :], 0)
        part = dot_nt(hot, cov_ref[:, k * cols:(k + 1) * cols]).astype(BF)
        for b in range(out_ref.shape[0]):
            out_ref[b, k * SLOT:(k + 1) * SLOT, :] = part[b * SLOT:(b + 1) * SLOT]


def sort_columns(cov, slots, blocks, per_step=32):
    rows, width = cov.shape
    ranges, cols = slots.shape
    return pl.pallas_call(
        functools.partial(sort_kernel, per_step),
        grid=(ranges // per_step,),
        in_specs=[
            pl.BlockSpec(slots.shape, lambda i: (0, 0)),
            pl.BlockSpec((rows, per_step * cols), lambda i: (0, i)),
        ],
        out_specs=pl.BlockSpec((blocks, per_step * SLOT, rows), lambda i: (0, i, 0)),
        out_shape=jax.ShapeDtypeStruct((blocks, ranges * SLOT, rows), BF),
        cost_estimate=pl.CostEstimate(flops=12 << 30, bytes_accessed=32 << 20, transcendentals=0),
        name="sort_columns",
    )(slots, cov)


def pack_kernel(first_ref, count_ref, dev_ref, slots_ref, table_ref, data_ref, out_ref, acc):
    block = pl.program_id(0)
    blocks, group, _, width = out_ref.shape
    windows = width // WIN
    rows_hot = one_hot(slots_ref[pl.ds(dev_ref[0], 1), :], 0)

    def part(first, base):
        start, hot = window_hot(table_ref, (block,), first, base)
        at = pl.multiple_of(start * LANES, LANES)
        return dot(hot, data_ref[0, pl.ds(at, REACH * LANES), :]).astype(BF)

    for job in range(group * windows):
        tile = block * group + job // windows
        acc[job * WIN:(job + 1) * WIN, :] = part(first_ref[tile, job % windows], job * WIN)

    def extra(job, carry):
        tile, w = block * group + job // windows, lax.rem(job, windows)
        at = pl.multiple_of(job * WIN, WIN)

        def more(i, carry):
            acc[pl.ds(at, WIN), :] += part(first_ref[tile, w] + i * REACH, at)
            return carry

        return lax.fori_loop(1, count_ref[tile, w], more, carry)

    most = count_ref[block * group, 0]
    for job in range(1, group * windows):
        most = jnp.maximum(most, count_ref[block * group + job // windows, job % windows])

    @pl.when(most > 1)
    def _():
        lax.fori_loop(0, group * windows, extra, 0)

    for g in range(group):
        out = dot_nt(rows_hot, acc[g * width:(g + 1) * width, :]).astype(BF)
        for b in range(blocks):
            out_ref[b, g] = out[b * SLOT:(b + 1) * SLOT]


def pack_columns(data, slots, table, firsts, counts, device, tile_cols):
    blocks, length, rows = data.shape
    tiles = firsts.shape[0]
    group = tiles // blocks
    grid_spec = pltpu.PrefetchScalarGridSpec(
        num_scalar_prefetch=3,
        grid=(blocks,),
        in_specs=[
            pl.BlockSpec(slots.shape, lambda i, f, n, d: (0, 0)),
            pl.BlockSpec(table.shape, lambda i, f, n, d: (0, 0, 0)),
            pl.BlockSpec((1, length, rows), lambda i, f, n, d: (i, 0, 0)),
        ],
        out_specs=pl.BlockSpec((blocks, group, SLOT, tile_cols), lambda i, f, n, d: (0, i, 0, 0)),
        scratch_shapes=[pltpu.VMEM((group * tile_cols, rows), BF)],
    )
    return pl.pallas_call(
        pack_kernel,
        grid_spec=grid_spec,
        out_shape=jax.ShapeDtypeStruct((blocks, tiles, SLOT, tile_cols), BF),
        cost_estimate=pl.CostEstimate(flops=12 << 30, bytes_accessed=24 << 20, transcendentals=0),
        name="pack_columns",
    )(firsts, counts, device, slots, table, data)


def load_lhs(z, u_ref, lhs, sems):
    rows, cols = u_ref.shape[1:]
    return [
        pltpu.make_async_copy(
            u_ref.at[4 * z + 2 * half + core],
            lhs.at[pl.ds(core * rows, rows), pl.ds(half * cols, cols)],
            sems.at[2 * half + core],
        )
        for half in range(2) for core in range(2)
    ]


def start_loads(steps, pos_ref, u_ref, lhs, sems):
    jobs = []
    for n, step in enumerate(steps):
        jobs.append(load_lhs(lax.rem(pos_ref[0] + step, 4), u_ref, lhs.at[n], sems.at[n]))
        for copy in jobs[n]:
            copy.start()
    return jobs


def multiply(jobs, lhs, tile_ref, core, keep_ref, give_ref):
    half = keep_ref.shape[2]
    give = pl.multiple_of((1 - core) * half, half)
    keep = pl.multiple_of(core * half, half)
    for n, copies in enumerate(jobs):
        for copy in copies:
            copy.wait()
        give_ref[n] = dot(lhs[n], tile_ref[:, pl.ds(give, half)])
        keep_ref[n] = dot(lhs[n], tile_ref[:, pl.ds(keep, half)])


def first_kernel(steps, pos_ref, first_ref, count_ref, table_ref, got_ref, u_ref,
                 tile_ref, keep_ref, give_ref, held, lhs, got_sem, lhs_sems):
    z, core = pos_ref[0], pos_ref[1]
    load = pltpu.make_async_copy(got_ref, held, got_sem)
    load.start()
    jobs = start_loads(steps, pos_ref, u_ref, lhs, lhs_sems)
    per_line = LANES // SLOT
    span = REACH * per_line
    windows = tile_ref.shape[0] // WIN
    block = 2 * z + core

    def part(first, base):
        start, hot = window_hot(table_ref, (block,), first, base)
        data = held[pl.ds(start * per_line, span)].reshape(REACH * LANES, held.shape[-1])
        return dot(hot, data).astype(BF)

    load.wait()
    for w in range(windows):
        tile, v = 2 * block + w // (windows // 2), w % (windows // 2)
        tile_ref[w * WIN:(w + 1) * WIN, :] = part(first_ref[tile, v], w * WIN)

    def window(w, carry):
        tile, v = 2 * block + w // (windows // 2), lax.rem(w, windows // 2)
        at = pl.multiple_of(w * WIN, WIN)

        def more(i, carry):
            tile_ref[pl.ds(at, WIN), :] += part(first_ref[tile, v] + i * REACH, at)
            return carry

        return lax.fori_loop(1, count_ref[tile, v], more, carry)

    lax.fori_loop(0, windows, window, 0)
    multiply(jobs, lhs, tile_ref, core, keep_ref, give_ref)


def next_kernel(steps, pos_ref, u_ref, tile_ref, keep_ref, give_ref, lhs, sems):
    jobs = start_loads(steps, pos_ref, u_ref, lhs, sems)
    multiply(jobs, lhs, tile_ref, pos_ref[1], keep_ref, give_ref)


def first_shares(steps, position, firsts, counts, table, received, u_block):
    owners, _, cols = received.shape
    rows, depth = 2 * u_block.shape[1], 2 * u_block.shape[2]
    smem = pl.BlockSpec(memory_space=pltpu.SMEM)
    vmem = pl.BlockSpec(memory_space=pltpu.VMEM)
    hbm = pl.BlockSpec(memory_space=pl.ANY)
    share = jax.ShapeDtypeStruct((len(steps), rows, cols // 2), F32)
    return pl.pallas_call(
        functools.partial(first_kernel, steps),
        in_specs=[smem, smem, smem, vmem, hbm, hbm],
        out_specs=(vmem, vmem, vmem),
        out_shape=(pltpu.VMEM((depth, cols), BF), share, share),
        scratch_shapes=[
            pltpu.VMEM((owners, SLOT, cols), BF),
            pltpu.VMEM((len(steps), rows, depth), BF),
            pltpu.SemaphoreType.DMA,
            pltpu.SemaphoreType.DMA((len(steps), 4)),
        ],
        cost_estimate=pl.CostEstimate(flops=24 << 30, bytes_accessed=24 << 20, transcendentals=0),
        compiler_params=pltpu.CompilerParams(vmem_limit_bytes=36 << 20),
        name="squeeze_and_first_shares",
    )(position, firsts, counts, table, received, u_block)


def next_shares(steps, position, u_block, tile):
    depth, cols = tile.shape
    rows = 2 * u_block.shape[1]
    smem = pl.BlockSpec(memory_space=pltpu.SMEM)
    vmem = pl.BlockSpec(memory_space=pltpu.VMEM)
    hbm = pl.BlockSpec(memory_space=pl.ANY)
    share = jax.ShapeDtypeStruct((len(steps), rows, cols // 2), F32)
    return pl.pallas_call(
        functools.partial(next_kernel, steps),
        in_specs=[smem, hbm, vmem],
        out_specs=(vmem, vmem),
        out_shape=(share, share),
        scratch_shapes=[
            pltpu.VMEM((len(steps), rows, depth), BF),
            pltpu.SemaphoreType.DMA((len(steps), 4)),
        ],
        cost_estimate=pl.CostEstimate(flops=12 << 30, bytes_accessed=16 << 20, transcendentals=0),
        compiler_params=pltpu.CompilerParams(vmem_limit_bytes=24 << 20),
        name="next_shares",
    )(position, u_block, tile)


def pairs(target):
    result = []
    for r in range(8):
        for c in range(16):
            z, core, y, x = target(r // 2, r % 2, c // 4, c % 4)
            result.append((r * 16 + c, (2 * z + core) * 16 + 4 * y + x))
    return result


def local(parent_cov, anc_index, fac_rows, inv_factor, own_inverse):
    row_count = lax.axis_size("row")
    col_count = lax.axis_size("col")
    owners = row_count * col_count
    parent_rows = parent_cov.shape[0]
    tile_cols = anc_index.shape[0] // col_count
    sep_cols = inv_factor.shape[1]
    row_index = lax.axis_index("row")
    col_index = lax.axis_index("col")
    core = row_index % 2
    device = jnp.reshape(row_index * col_count + col_index, (1,)).astype(I32)
    position = jnp.stack([row_index // 2, core]).astype(I32)
    both = ("row", "col")
    swap = pairs(lambda z, core, y, x: (z, 1 - core, y, x))

    own_ids = lax.dynamic_slice_in_dim(anc_index, col_index * tile_cols, tile_cols)
    rank = jnp.sum((own_ids[None, :] < own_ids[:, None]).astype(I32), axis=1)
    perm = (jnp.arange(tile_cols, dtype=I32)[:, None] == rank[None, :]).astype(BF)
    row_ids = jnp.arange(inv_factor.shape[0], dtype=I32)[:, None]
    col_ids = row_index * sep_cols + jnp.arange(sep_cols, dtype=I32)[None, :]
    lower = jnp.where(row_ids >= col_ids, inv_factor, jnp.zeros((), inv_factor.dtype))
    u_tile = jnp.dot(fac_rows, lower, preferred_element_type=F32).astype(BF)
    u_t = lax.dot_general(
        u_tile, perm, (((0,), (1,)), ((), ())), preferred_element_type=F32
    ).astype(BF)
    piece = lax.ppermute(
        u_t, both, pairs(lambda z, core, y, x: (y, x // 2, z, 2 * (x % 2) + core))
    )
    slots, table, firsts, counts = index_tables(anc_index, owners, parent_rows, col_count)
    data = sort_columns(parent_cov, slots, row_count)
    piece, data = lax.optimization_barrier((piece, data))
    u_block = lax.all_gather(piece, "col", axis=0)
    outgoing = pack_columns(data, slots, table, firsts, counts, device, tile_cols)
    outgoing, u_t = lax.optimization_barrier((outgoing, u_t))
    u_cols = lax.all_gather(u_t, "row", axis=0, tiled=True)
    flat_out = outgoing.reshape(owners * SLOT, tile_cols)
    received = lax.all_to_all(flat_out, both, split_axis=0, concat_axis=0, tiled=True)
    received = received.reshape(owners, SLOT, tile_cols)

    tile, keep, give = first_shares((2, 1), position, firsts, counts, table, received, u_block)
    first = (keep + lax.ppermute(give, both, swap)).astype(BF)
    keep, give = next_shares((3, 0), position, u_block, tile)
    second = keep + lax.ppermute(give, both, swap)
    total = second[1]
    for step, share in ((2, first[0]), (1, first[1]), (3, second[0].astype(BF))):
        share = lax.ppermute(
            share, both, pairs(lambda z, core, y, x, step=step: ((z + step) % 4, core, y, x))
        )
        total = total + share.astype(F32)
    total = -total
    kept = lax.dynamic_slice_in_dim(total, core * sep_cols, sep_cols, axis=0)
    given = lax.dynamic_slice_in_dim(total, (1 - core) * sep_cols, sep_cols, axis=0)
    taken = lax.ppermute(given, both, swap)
    sa_sorted = jnp.concatenate(
        [jnp.where(core == 0, kept, taken), jnp.where(core == 0, taken, kept)], axis=1
    )

    sa_high = sa_sorted.astype(BF)
    ss_part = dot_nt(u_cols, sa_high).astype(BF)
    ss_all = lax.all_to_all(ss_part, "col", split_axis=0, concat_axis=0, tiled=True)
    sa_low = (sa_sorted - sa_high.astype(F32)).astype(BF)
    cov_sa = dot(sa_high, perm) + dot(sa_low, perm)
    ss_sum = jnp.sum(ss_all.reshape(col_count, -1, ss_all.shape[1]).astype(F32), axis=0)
    cov_ss = own_inverse - ss_sum.T
    return (cov_sa, cov_ss)


def solution(mesh):
    return jax.shard_map(
        local,
        mesh=mesh,
        in_specs=(P(("row", "col"), None), P(), P("col", None), P(None, "row"), P("row", "col")),
        out_specs=(P("row", "col"), P("row", "col")),
        check_vma=False,
    )
```

```python
import functools

import jax
import jax.numpy as jnp
from jax import lax
from jax.experimental import pallas as pl
from jax.experimental.pallas import tpu as pltpu
from jax.sharding import PartitionSpec as P

BF = jnp.bfloat16
F32 = jnp.float32
I32 = jnp.int32
SLOT = 32
LANES = 128
REACH = 10
LINES = 32
WIN = 256

def dot_nt(a, b):
    return lax.dot_general(a, b, (((1,), (1,)), ((), ())), preferred_element_type=F32)


def dot(a, b):
    return jnp.dot(a, b, preferred_element_type=F32)


def iota(shape, axis):
    return lax.broadcasted_iota(I32, shape, axis)


def ones_where(cond):
    return jnp.where(cond, 1.0, 0.0).astype(BF)


def index_kernel(tiles, anc_ref, slots_ref, table_ref, first_ref, count_ref):
    owners, rows = slots_ref.shape
    chunk = anc_ref.shape[1]
    tile_of = jnp.zeros((owners, rows), F32)
    for j in range(anc_ref.shape[0]):
        ids = anc_ref[j:j + 1, :]
        owner, inner = ids // rows, ids % rows
        tile = ((iota((1, chunk), 1) + j * chunk) // (anc_ref.shape[0] * chunk // tiles) + 1).astype(F32)
        owner_hot = jnp.where(iota((owners, chunk), 0) == owner, tile, 0.0).astype(BF)
        inner_hot = ones_where(iota((rows, chunk), 0) == inner)
        tile_of = tile_of + dot_nt(owner_hot, inner_hot)
    at = iota((rows, rows + LANES), 1)
    before = ones_where((iota((rows, rows + LANES), 0) < at) | (at >= rows))
    below = ones_where(iota((owners, owners), 1) < iota((owners, owners), 0))
    per_line = LANES // SLOT
    lines = owners // per_line
    pick = ones_where(iota((lines, owners), 1) // per_line == iota((lines, owners), 0))
    spread = iota((owners, LANES), 0) % per_line == iota((owners, LANES), 1) // SLOT
    s = (iota((lines, LANES), 1) % SLOT).astype(F32)
    edge = (iota((owners, LANES), 1) * WIN).astype(F32)
    spread = jnp.concatenate([spread] * tiles, axis=1)
    edge = jnp.concatenate([edge] * tiles, axis=1)

    def expand(v):
        return dot(pick, jnp.where(spread, v, 0.0).astype(BF))

    masks = [tile_of == float(c + 1) for c in range(tiles)]
    both = dot(jnp.concatenate([ones_where(mask) for mask in masks], axis=0), before)
    ahead = [both[c * owners:(c + 1) * owners, :rows] for c in range(tiles)]
    numbers = [both[c * owners:(c + 1) * owners, rows:] for c in range(tiles)]
    slots = jnp.zeros((owners, rows), F32) - 1.0
    for c in range(tiles):
        lift = ahead[c] + float(c // 2 * SLOT + 1)
        if c % 2:
            lift = lift + jnp.concatenate([numbers[c - 1]] * (rows // LANES), axis=1)
        slots = slots + jnp.where(masks[c], lift, 0.0)
    slots_ref[...] = slots.astype(I32)
    number = jnp.concatenate(numbers, axis=1)
    start = dot(below, number.astype(BF))
    end = start + number
    lead = jnp.sum(jnp.where(end <= edge, 1.0, 0.0), axis=0, keepdims=True).astype(I32)
    last = jnp.sum(jnp.where(start < edge + float(WIN), 1.0, 0.0), axis=0, keepdims=True).astype(I32) - 1
    first = lead // per_line
    count = (last // per_line - first) // REACH + 1
    high = jnp.floor(start * (1.0 / 32.0))
    n = expand(number)
    p = expand(high) * 32.0 + expand(start - high * 32.0)
    tile_len = float(anc_ref.shape[0] * chunk // tiles)
    for c in range(tiles):
        at = slice(c * LANES, (c + 1) * LANES)
        first_ref[c:c + 1, :] = first[:, at]
        count_ref[c:c + 1, :] = count[:, at]
        if c % 2:
            old = slice((c - 1) * LANES, c * LANES)
            n0, p0 = n[:, old], p[:, old]
            to = jnp.where(s < n0, p0 + s, jnp.where(s < n0 + n[:, at], tile_len + p[:, at] + s - n0, -1.0))
            table_ref[c // 2, 0:lines, :] = to.astype(I32)


def index_tables(anc, owners, rows, tiles):
    lines = owners * SLOT // LANES
    return pl.pallas_call(
        functools.partial(index_kernel, tiles),
        out_shape=(
            jax.ShapeDtypeStruct((owners, rows), I32),
            jax.ShapeDtypeStruct((tiles // 2, lines, LANES), I32),
            jax.ShapeDtypeStruct((tiles, LANES), I32),
            jax.ShapeDtypeStruct((tiles, LANES), I32),
        ),
        cost_estimate=pl.CostEstimate(flops=8 << 30, bytes_accessed=1 << 20, transcendentals=0),
        name="index_tables",
    )(anc.reshape(-1, 2048))


def one_hot(targets, base):
    ids = iota((WIN, targets.shape[-1]), 0) + base
    return ones_where(ids == targets)


def window_hot(table, lead, first, base):
    start = jnp.minimum(first, LINES - REACH)
    lines = []
    for i in range(REACH):
        line = table[lead + (pl.ds(start + i, 1), slice(None))]
        lines.append(one_hot(jnp.where(start + i < first, -1, line), base))
    return start, jnp.concatenate(lines, axis=1)


def sort_kernel(per_step, slots_ref, cov_ref, out_ref):
    cols = slots_ref.shape[-1]
    for k in range(per_step):
        hot = one_hot(slots_ref[pl.ds(pl.program_id(0) * per_step + k, 1), :], 0)
        part = dot_nt(hot, cov_ref[:, k * cols:(k + 1) * cols]).astype(BF)
        for b in range(out_ref.shape[0]):
            out_ref[b, k * SLOT:(k + 1) * SLOT, :] = part[b * SLOT:(b + 1) * SLOT]


def sort_columns(cov, slots, blocks, per_step=32):
    rows, width = cov.shape
    ranges, cols = slots.shape
    return pl.pallas_call(
        functools.partial(sort_kernel, per_step),
        grid=(ranges // per_step,),
        in_specs=[
            pl.BlockSpec(slots.shape, lambda i: (0, 0)),
            pl.BlockSpec((rows, per_step * cols), lambda i: (0, i)),
        ],
        out_specs=pl.BlockSpec((blocks, per_step * SLOT, rows), lambda i: (0, i, 0)),
        out_shape=jax.ShapeDtypeStruct((blocks, ranges * SLOT, rows), BF),
        cost_estimate=pl.CostEstimate(flops=12 << 30, bytes_accessed=32 << 20, transcendentals=0),
        name="sort_columns",
    )(slots, cov)


def pack_kernel(first_ref, count_ref, dev_ref, slots_ref, table_ref, data_ref, out_ref, acc):
    block = pl.program_id(0)
    blocks, group, _, width = out_ref.shape
    windows = width // WIN
    rows_hot = one_hot(slots_ref[pl.ds(dev_ref[0], 1), :], 0)

    def part(first, base):
        start, hot = window_hot(table_ref, (block,), first, base)
        at = pl.multiple_of(start * LANES, LANES)
        return dot(hot, data_ref[0, pl.ds(at, REACH * LANES), :]).astype(BF)

    for job in range(group * windows):
        tile = block * group + job // windows
        acc[job * WIN:(job + 1) * WIN, :] = part(first_ref[tile, job % windows], job * WIN)

    def extra(job, carry):
        tile, w = block * group + job // windows, lax.rem(job, windows)
        at = pl.multiple_of(job * WIN, WIN)

        def more(i, carry):
            acc[pl.ds(at, WIN), :] += part(first_ref[tile, w] + i * REACH, at)
            return carry

        return lax.fori_loop(1, count_ref[tile, w], more, carry)

    most = count_ref[block * group, 0]
    for job in range(1, group * windows):
        most = jnp.maximum(most, count_ref[block * group + job // windows, job % windows])

    @pl.when(most > 1)
    def _():
        lax.fori_loop(0, group * windows, extra, 0)

    for g in range(group):
        out = dot_nt(rows_hot, acc[g * width:(g + 1) * width, :]).astype(BF)
        for b in range(blocks):
            out_ref[b, g] = out[b * SLOT:(b + 1) * SLOT]


def pack_columns(data, slots, table, firsts, counts, device, tile_cols):
    blocks, length, rows = data.shape
    tiles = firsts.shape[0]
    group = tiles // blocks
    grid_spec = pltpu.PrefetchScalarGridSpec(
        num_scalar_prefetch=3,
        grid=(blocks,),
        in_specs=[
            pl.BlockSpec(slots.shape, lambda i, f, n, d: (0, 0)),
            pl.BlockSpec(table.shape, lambda i, f, n, d: (0, 0, 0)),
            pl.BlockSpec((1, length, rows), lambda i, f, n, d: (i, 0, 0)),
        ],
        out_specs=pl.BlockSpec((blocks, group, SLOT, tile_cols), lambda i, f, n, d: (0, i, 0, 0)),
        scratch_shapes=[pltpu.VMEM((group * tile_cols, rows), BF)],
    )
    return pl.pallas_call(
        pack_kernel,
        grid_spec=grid_spec,
        out_shape=jax.ShapeDtypeStruct((blocks, tiles, SLOT, tile_cols), BF),
        cost_estimate=pl.CostEstimate(flops=12 << 30, bytes_accessed=24 << 20, transcendentals=0),
        name="pack_columns",
    )(firsts, counts, device, slots, table, data)


def load_lhs(z, u_ref, lhs, sems):
    rows, cols = u_ref.shape[1:]
    return [
        pltpu.make_async_copy(
            u_ref.at[4 * z + 2 * half + core],
            lhs.at[pl.ds(core * rows, rows), pl.ds(half * cols, cols)],
            sems.at[2 * half + core],
        )
        for half in range(2) for core in range(2)
    ]


def start_loads(steps, pos_ref, u_ref, lhs, sems):
    jobs = []
    for n, step in enumerate(steps):
        jobs.append(load_lhs(lax.rem(pos_ref[0] + step, 4), u_ref, lhs.at[n], sems.at[n]))
        for copy in jobs[n]:
            copy.start()
    return jobs


def multiply(jobs, lhs, tile_ref, core, keep_ref, give_ref):
    half = keep_ref.shape[2]
    give = pl.multiple_of((1 - core) * half, half)
    keep = pl.multiple_of(core * half, half)
    for copies in jobs:
        for copy in copies:
            copy.wait()

    def product(n, carry):
        give_ref[n] = dot(lhs[n], tile_ref[:, pl.ds(give, half)])
        keep_ref[n] = dot(lhs[n], tile_ref[:, pl.ds(keep, half)])
        return carry

    lax.fori_loop(0, len(jobs), product, 0)


def first_kernel(steps, pos_ref, first_ref, count_ref, table_ref, got_ref, u_ref,
                 tile_ref, keep_ref, give_ref, held, lhs, got_sem, lhs_sems):
    z, core = pos_ref[0], pos_ref[1]
    load = pltpu.make_async_copy(got_ref, held, got_sem)
    load.start()
    jobs = start_loads(steps, pos_ref, u_ref, lhs, lhs_sems)
    per_line = LANES // SLOT
    span = REACH * per_line
    windows = tile_ref.shape[0] // WIN
    block = 2 * z + core

    def part(first, base):
        start, hot = window_hot(table_ref, (block,), first, base)
        data = held[pl.ds(start * per_line, span)].reshape(REACH * LANES, held.shape[-1])
        return dot(hot, data).astype(BF)

    load.wait()
    for w in range(windows):
        tile, v = 2 * block + w // (windows // 2), w % (windows // 2)
        tile_ref[w * WIN:(w + 1) * WIN, :] = part(first_ref[tile, v], w * WIN)

    def window(w, carry):
        tile, v = 2 * block + w // (windows // 2), lax.rem(w, windows // 2)
        at = pl.multiple_of(w * WIN, WIN)

        def more(i, carry):
            tile_ref[pl.ds(at, WIN), :] += part(first_ref[tile, v] + i * REACH, at)
            return carry

        return lax.fori_loop(1, count_ref[tile, v], more, carry)

    lax.fori_loop(0, windows, window, 0)
    multiply(jobs, lhs, tile_ref, core, keep_ref, give_ref)


def next_kernel(steps, pos_ref, u_ref, tile_ref, keep_ref, give_ref, lhs, sems):
    jobs = start_loads(steps, pos_ref, u_ref, lhs, sems)
    multiply(jobs, lhs, tile_ref, pos_ref[1], keep_ref, give_ref)


def first_shares(steps, position, firsts, counts, table, received, u_block):
    owners, _, cols = received.shape
    rows, depth = 2 * u_block.shape[1], 2 * u_block.shape[2]
    smem = pl.BlockSpec(memory_space=pltpu.SMEM)
    vmem = pl.BlockSpec(memory_space=pltpu.VMEM)
    hbm = pl.BlockSpec(memory_space=pl.ANY)
    share = jax.ShapeDtypeStruct((len(steps), rows, cols // 2), F32)
    return pl.pallas_call(
        functools.partial(first_kernel, steps),
        in_specs=[smem, smem, smem, vmem, hbm, hbm],
        out_specs=(vmem, vmem, vmem),
        out_shape=(pltpu.VMEM((depth, cols), BF), share, share),
        scratch_shapes=[
            pltpu.VMEM((owners, SLOT, cols), BF),
            pltpu.VMEM((len(steps), rows, depth), BF),
            pltpu.SemaphoreType.DMA,
            pltpu.SemaphoreType.DMA((len(steps), 4)),
        ],
        cost_estimate=pl.CostEstimate(flops=24 << 30, bytes_accessed=24 << 20, transcendentals=0),
        compiler_params=pltpu.CompilerParams(vmem_limit_bytes=36 << 20),
        name="squeeze_and_first_shares",
    )(position, firsts, counts, table, received, u_block)


def next_shares(steps, position, u_block, tile):
    depth, cols = tile.shape
    rows = 2 * u_block.shape[1]
    smem = pl.BlockSpec(memory_space=pltpu.SMEM)
    vmem = pl.BlockSpec(memory_space=pltpu.VMEM)
    hbm = pl.BlockSpec(memory_space=pl.ANY)
    share = jax.ShapeDtypeStruct((len(steps), rows, cols // 2), F32)
    return pl.pallas_call(
        functools.partial(next_kernel, steps),
        in_specs=[smem, hbm, vmem],
        out_specs=(vmem, vmem),
        out_shape=(share, share),
        scratch_shapes=[
            pltpu.VMEM((len(steps), rows, depth), BF),
            pltpu.SemaphoreType.DMA((len(steps), 4)),
        ],
        cost_estimate=pl.CostEstimate(flops=12 << 30, bytes_accessed=16 << 20, transcendentals=0),
        compiler_params=pltpu.CompilerParams(vmem_limit_bytes=24 << 20),
        name="next_shares",
    )(position, u_block, tile)


def pairs(target):
    result = []
    for r in range(8):
        for c in range(16):
            z, core, y, x = target(r // 2, r % 2, c // 4, c % 4)
            result.append((r * 16 + c, (2 * z + core) * 16 + 4 * y + x))
    return result


def local(parent_cov, anc_index, fac_rows, inv_factor, own_inverse):
    row_count = lax.axis_size("row")
    col_count = lax.axis_size("col")
    owners = row_count * col_count
    parent_rows = parent_cov.shape[0]
    tile_cols = anc_index.shape[0] // col_count
    sep_cols = inv_factor.shape[1]
    row_index = lax.axis_index("row")
    col_index = lax.axis_index("col")
    core = row_index % 2
    device = jnp.reshape(row_index * col_count + col_index, (1,)).astype(I32)
    position = jnp.stack([row_index // 2, core]).astype(I32)
    both = ("row", "col")
    swap = pairs(lambda z, core, y, x: (z, 1 - core, y, x))

    own_ids = lax.dynamic_slice_in_dim(anc_index, col_index * tile_cols, tile_cols)
    rank = jnp.sum((own_ids[None, :] < own_ids[:, None]).astype(I32), axis=1)
    perm = (jnp.arange(tile_cols, dtype=I32)[:, None] == rank[None, :]).astype(BF)
    row_ids = jnp.arange(inv_factor.shape[0], dtype=I32)[:, None]
    col_ids = row_index * sep_cols + jnp.arange(sep_cols, dtype=I32)[None, :]
    lower = jnp.where(row_ids >= col_ids, inv_factor, jnp.zeros((), inv_factor.dtype))
    u_tile = jnp.dot(fac_rows, lower, preferred_element_type=F32).astype(BF)
    u_t = lax.dot_general(
        u_tile, perm, (((0,), (1,)), ((), ())), preferred_element_type=F32
    ).astype(BF)
    piece = lax.ppermute(
        u_t, both, pairs(lambda z, core, y, x: (y, x // 2, z, 2 * (x % 2) + core))
    )
    slots, table, firsts, counts = index_tables(anc_index, owners, parent_rows, col_count)
    data = sort_columns(parent_cov, slots, row_count)
    piece, data = lax.optimization_barrier((piece, data))
    u_block = lax.all_gather(piece, "col", axis=0)
    outgoing = pack_columns(data, slots, table, firsts, counts, device, tile_cols)
    outgoing, u_t = lax.optimization_barrier((outgoing, u_t))
    u_cols = lax.all_gather(u_t, "row", axis=0, tiled=True)
    flat_out = outgoing.reshape(owners * SLOT, tile_cols)
    received = lax.all_to_all(flat_out, both, split_axis=0, concat_axis=0, tiled=True)
    received = received.reshape(owners, SLOT, tile_cols)

    tile, keep, give = first_shares((2, 1), position, firsts, counts, table, received, u_block)
    first = (keep + lax.ppermute(give, both, swap)).astype(BF)
    keep, give = next_shares((3, 0), position, u_block, tile)
    second = keep + lax.ppermute(give, both, swap)
    total = second[1]
    for step, share in ((2, first[0]), (1, first[1]), (3, second[0].astype(BF))):
        share = lax.ppermute(
            share, both, pairs(lambda z, core, y, x, step=step: ((z + step) % 4, core, y, x))
        )
        total = total + share.astype(F32)
    total = -total
    kept = lax.dynamic_slice_in_dim(total, core * sep_cols, sep_cols, axis=0)
    given = lax.dynamic_slice_in_dim(total, (1 - core) * sep_cols, sep_cols, axis=0)
    taken = lax.ppermute(given, both, swap)
    sa_sorted = jnp.concatenate(
        [jnp.where(core == 0, kept, taken), jnp.where(core == 0, taken, kept)], axis=1
    )

    sa_high = sa_sorted.astype(BF)
    ss_part = dot_nt(u_cols, sa_high).astype(BF)
    ss_all = lax.all_to_all(ss_part, "col", split_axis=0, concat_axis=0, tiled=True)
    sa_low = (sa_sorted - sa_high.astype(F32)).astype(BF)
    cov_sa = dot(sa_high, perm) + dot(sa_low, perm)
    ss_sum = jnp.sum(ss_all.reshape(col_count, -1, ss_all.shape[1]).astype(F32), axis=0)
    cov_ss = own_inverse - ss_sum.T
    return (cov_sa, cov_ss)


def solution(mesh):
    return jax.shard_map(
        local,
        mesh=mesh,
        in_specs=(P(("row", "col"), None), P(), P("col", None), P(None, "row"), P("row", "col")),
        out_specs=(P("row", "col"), P("row", "col")),
        check_vma=False,
    )
```

```python
import functools

import jax
import jax.numpy as jnp
from jax import lax
from jax.experimental import pallas as pl
from jax.experimental.pallas import tpu as pltpu
from jax.sharding import PartitionSpec as P

BF = jnp.bfloat16
F32 = jnp.float32
I32 = jnp.int32
SLOT = 32
LANES = 128
REACH = 10
LINES = 32
WIN = 256

def dot_nt(a, b):
    return lax.dot_general(a, b, (((1,), (1,)), ((), ())), preferred_element_type=F32)


def dot(a, b):
    return jnp.dot(a, b, preferred_element_type=F32)


def iota(shape, axis):
    return lax.broadcasted_iota(I32, shape, axis)


def ones_where(cond):
    return jnp.where(cond, 1.0, 0.0).astype(BF)


def index_kernel(tiles, anc_ref, slots_ref, table_ref, first_ref, count_ref):
    owners, rows = slots_ref.shape
    chunk = anc_ref.shape[1]
    tile_of = jnp.zeros((owners, rows), F32)
    for j in range(anc_ref.shape[0]):
        ids = anc_ref[j:j + 1, :]
        owner, inner = ids // rows, ids % rows
        tile = ((iota((1, chunk), 1) + j * chunk) // (anc_ref.shape[0] * chunk // tiles) + 1).astype(F32)
        owner_hot = jnp.where(iota((owners, chunk), 0) == owner, tile, 0.0).astype(BF)
        inner_hot = ones_where(iota((rows, chunk), 0) == inner)
        tile_of = tile_of + dot_nt(owner_hot, inner_hot)
    at = iota((rows, rows + LANES), 1)
    before = ones_where((iota((rows, rows + LANES), 0) < at) | (at >= rows))
    below = ones_where(iota((owners, owners), 1) < iota((owners, owners), 0))
    per_line = LANES // SLOT
    lines = owners // per_line
    pick = ones_where(iota((lines, owners), 1) // per_line == iota((lines, owners), 0))
    spread = iota((owners, LANES), 0) % per_line == iota((owners, LANES), 1) // SLOT
    s = (iota((lines, LANES), 1) % SLOT).astype(F32)
    edge = (iota((owners, LANES), 1) * WIN).astype(F32)
    spread = jnp.concatenate([spread] * tiles, axis=1)
    edge = jnp.concatenate([edge] * tiles, axis=1)

    def expand(v):
        return dot(pick, jnp.where(spread, v, 0.0).astype(BF))

    masks = [tile_of == float(c + 1) for c in range(tiles)]
    both = dot(jnp.concatenate([ones_where(mask) for mask in masks], axis=0), before)
    ahead = [both[c * owners:(c + 1) * owners, :rows] for c in range(tiles)]
    numbers = [both[c * owners:(c + 1) * owners, rows:] for c in range(tiles)]
    slots = jnp.zeros((owners, rows), F32) - 1.0
    for c in range(tiles):
        lift = ahead[c] + float(c // 2 * SLOT + 1)
        if c % 2:
            lift = lift + jnp.concatenate([numbers[c - 1]] * (rows // LANES), axis=1)
        slots = slots + jnp.where(masks[c], lift, 0.0)
    slots_ref[...] = slots.astype(I32)
    number = jnp.concatenate(numbers, axis=1)
    start = dot(below, number.astype(BF))
    end = start + number
    lead = jnp.sum(jnp.where(end <= edge, 1.0, 0.0), axis=0, keepdims=True).astype(I32)
    last = jnp.sum(jnp.where(start < edge + float(WIN), 1.0, 0.0), axis=0, keepdims=True).astype(I32) - 1
    first = lead // per_line
    count = (last // per_line - first) // REACH + 1
    high = jnp.floor(start * (1.0 / 32.0))
    n = expand(number)
    p = expand(high) * 32.0 + expand(start - high * 32.0)
    tile_len = float(anc_ref.shape[0] * chunk // tiles)
    for c in range(tiles):
        at = slice(c * LANES, (c + 1) * LANES)
        first_ref[c:c + 1, :] = first[:, at]
        count_ref[c:c + 1, :] = count[:, at]
        if c % 2:
            old = slice((c - 1) * LANES, c * LANES)
            n0, p0 = n[:, old], p[:, old]
            to = jnp.where(s < n0, p0 + s, jnp.where(s < n0 + n[:, at], tile_len + p[:, at] + s - n0, -1.0))
            table_ref[c // 2, 0:lines, :] = to.astype(I32)


def index_tables(anc, owners, rows, tiles):
    lines = owners * SLOT // LANES
    return pl.pallas_call(
        functools.partial(index_kernel, tiles),
        out_shape=(
            jax.ShapeDtypeStruct((owners, rows), I32),
            jax.ShapeDtypeStruct((tiles // 2, lines, LANES), I32),
            jax.ShapeDtypeStruct((tiles, LANES), I32),
            jax.ShapeDtypeStruct((tiles, LANES), I32),
        ),
        cost_estimate=pl.CostEstimate(flops=8 << 30, bytes_accessed=1 << 20, transcendentals=0),
        name="index_tables",
    )(anc.reshape(-1, 2048))


def one_hot(targets, base):
    ids = iota((WIN, targets.shape[-1]), 0) + base
    return ones_where(ids == targets)


def window_hot(table, lead, first, base):
    start = jnp.minimum(first, LINES - REACH)
    lines = []
    for i in range(REACH):
        line = table[lead + (pl.ds(start + i, 1), slice(None))]
        lines.append(one_hot(jnp.where(start + i < first, -1, line), base))
    return start, jnp.concatenate(lines, axis=1)


def sort_kernel(per_step, slots_ref, cov_ref, out_ref):
    cols = slots_ref.shape[-1]
    for k in range(per_step):
        hot = one_hot(slots_ref[pl.ds(pl.program_id(0) * per_step + k, 1), :], 0)
        part = dot_nt(hot, cov_ref[:, k * cols:(k + 1) * cols]).astype(BF)
        for b in range(out_ref.shape[0]):
            out_ref[b, k * SLOT:(k + 1) * SLOT, :] = part[b * SLOT:(b + 1) * SLOT]


def sort_columns(cov, slots, blocks, per_step=32):
    rows, width = cov.shape
    ranges, cols = slots.shape
    return pl.pallas_call(
        functools.partial(sort_kernel, per_step),
        grid=(ranges // per_step,),
        in_specs=[
            pl.BlockSpec(slots.shape, lambda i: (0, 0)),
            pl.BlockSpec((rows, per_step * cols), lambda i: (0, i)),
        ],
        out_specs=pl.BlockSpec((blocks, per_step * SLOT, rows), lambda i: (0, i, 0)),
        out_shape=jax.ShapeDtypeStruct((blocks, ranges * SLOT, rows), BF),
        cost_estimate=pl.CostEstimate(flops=12 << 30, bytes_accessed=32 << 20, transcendentals=0),
        name="sort_columns",
    )(slots, cov)


def pack_kernel(first_ref, count_ref, dev_ref, slots_ref, table_ref, data_ref, out_ref, acc):
    block = pl.program_id(0)
    blocks, group, _, width = out_ref.shape
    windows = width // WIN
    rows_hot = one_hot(slots_ref[pl.ds(dev_ref[0], 1), :], 0)

    def part(first, base):
        start, hot = window_hot(table_ref, (block,), first, base)
        at = pl.multiple_of(start * LANES, LANES)
        return dot(hot, data_ref[0, pl.ds(at, REACH * LANES), :]).astype(BF)

    for job in range(group * windows):
        tile = block * group + job // windows
        acc[job * WIN:(job + 1) * WIN, :] = part(first_ref[tile, job % windows], job * WIN)

    def extra(job, carry):
        tile, w = block * group + job // windows, lax.rem(job, windows)
        at = pl.multiple_of(job * WIN, WIN)

        def more(i, carry):
            acc[pl.ds(at, WIN), :] += part(first_ref[tile, w] + i * REACH, at)
            return carry

        return lax.fori_loop(1, count_ref[tile, w], more, carry)

    most = count_ref[block * group, 0]
    for job in range(1, group * windows):
        most = jnp.maximum(most, count_ref[block * group + job // windows, job % windows])

    @pl.when(most > 1)
    def _():
        lax.fori_loop(0, group * windows, extra, 0)

    for g in range(group):
        out = dot_nt(rows_hot, acc[g * width:(g + 1) * width, :]).astype(BF)
        for b in range(blocks):
            out_ref[b, g] = out[b * SLOT:(b + 1) * SLOT]


def pack_columns(data, slots, table, firsts, counts, device, tile_cols):
    blocks, length, rows = data.shape
    tiles = firsts.shape[0]
    group = tiles // blocks
    grid_spec = pltpu.PrefetchScalarGridSpec(
        num_scalar_prefetch=3,
        grid=(blocks,),
        in_specs=[
            pl.BlockSpec(slots.shape, lambda i, f, n, d: (0, 0)),
            pl.BlockSpec(table.shape, lambda i, f, n, d: (0, 0, 0)),
            pl.BlockSpec((1, length, rows), lambda i, f, n, d: (i, 0, 0)),
        ],
        out_specs=pl.BlockSpec((blocks, group, SLOT, tile_cols), lambda i, f, n, d: (0, i, 0, 0)),
        scratch_shapes=[pltpu.VMEM((group * tile_cols, rows), BF)],
    )
    return pl.pallas_call(
        pack_kernel,
        grid_spec=grid_spec,
        out_shape=jax.ShapeDtypeStruct((blocks, tiles, SLOT, tile_cols), BF),
        cost_estimate=pl.CostEstimate(flops=12 << 30, bytes_accessed=24 << 20, transcendentals=0),
        name="pack_columns",
    )(firsts, counts, device, slots, table, data)


def load_lhs(z, u_ref, lhs, sems):
    rows, cols = u_ref.shape[1:]
    return [
        pltpu.make_async_copy(
            u_ref.at[4 * z + 2 * half + core],
            lhs.at[pl.ds(core * rows, rows), pl.ds(half * cols, cols)],
            sems.at[2 * half + core],
        )
        for half in range(2) for core in range(2)
    ]


def start_loads(steps, pos_ref, u_ref, lhs, sems):
    jobs = []
    for n, step in enumerate(steps):
        jobs.append(load_lhs(lax.rem(pos_ref[0] + step, 4), u_ref, lhs.at[n], sems.at[n]))
        for copy in jobs[n]:
            copy.start()
    return jobs


def multiply(jobs, lhs, tile_ref, core, keep_ref, give_ref):
    half = keep_ref.shape[2]
    give = pl.multiple_of((1 - core) * half, half)
    keep = pl.multiple_of(core * half, half)
    for copies in jobs:
        for copy in copies:
            copy.wait()

    def product(n, carry):
        give_ref[n] = dot(lhs[n], tile_ref[:, pl.ds(give, half)])
        keep_ref[n] = dot(lhs[n], tile_ref[:, pl.ds(keep, half)])
        return carry

    lax.fori_loop(0, len(jobs), product, 0)


def first_kernel(steps, pos_ref, first_ref, count_ref, table_ref, got_ref, u_ref,
                 tile_ref, keep_ref, give_ref, held, lhs, got_sem, lhs_sems):
    z, core = pos_ref[0], pos_ref[1]
    load = pltpu.make_async_copy(got_ref, held, got_sem)
    load.start()
    jobs = start_loads(steps, pos_ref, u_ref, lhs, lhs_sems)
    per_line = LANES // SLOT
    span = REACH * per_line
    windows = tile_ref.shape[0] // WIN
    block = 2 * z + core

    def part(first, base):
        start, hot = window_hot(table_ref, (block,), first, base)
        data = held[pl.ds(start * per_line, span)].reshape(REACH * LANES, held.shape[-1])
        return dot(hot, data).astype(BF)

    load.wait()
    for w in range(windows):
        tile, v = 2 * block + w // (windows // 2), w % (windows // 2)
        tile_ref[w * WIN:(w + 1) * WIN, :] = part(first_ref[tile, v], w * WIN)

    def window(w, carry):
        tile, v = 2 * block + w // (windows // 2), lax.rem(w, windows // 2)
        at = pl.multiple_of(w * WIN, WIN)

        def more(i, carry):
            tile_ref[pl.ds(at, WIN), :] += part(first_ref[tile, v] + i * REACH, at)
            return carry

        return lax.fori_loop(1, count_ref[tile, v], more, carry)

    lax.fori_loop(0, windows, window, 0)
    multiply(jobs, lhs, tile_ref, core, keep_ref, give_ref)


def next_kernel(steps, pos_ref, u_ref, tile_ref, keep_ref, give_ref, lhs, sems):
    jobs = start_loads(steps, pos_ref, u_ref, lhs, sems)
    multiply(jobs, lhs, tile_ref, pos_ref[1], keep_ref, give_ref)


def first_shares(steps, position, firsts, counts, table, received, u_block):
    owners, _, cols = received.shape
    rows, depth = 2 * u_block.shape[1], 2 * u_block.shape[2]
    smem = pl.BlockSpec(memory_space=pltpu.SMEM)
    vmem = pl.BlockSpec(memory_space=pltpu.VMEM)
    hbm = pl.BlockSpec(memory_space=pl.ANY)
    share = jax.ShapeDtypeStruct((len(steps), rows, cols // 2), F32)
    return pl.pallas_call(
        functools.partial(first_kernel, steps),
        in_specs=[smem, smem, smem, vmem, hbm, hbm],
        out_specs=(vmem, vmem, vmem),
        out_shape=(pltpu.VMEM((depth, cols), BF), share, share),
        scratch_shapes=[
            pltpu.VMEM((owners, SLOT, cols), BF),
            pltpu.VMEM((len(steps), rows, depth), BF),
            pltpu.SemaphoreType.DMA,
            pltpu.SemaphoreType.DMA((len(steps), 4)),
        ],
        cost_estimate=pl.CostEstimate(flops=24 << 30, bytes_accessed=24 << 20, transcendentals=0),
        compiler_params=pltpu.CompilerParams(vmem_limit_bytes=36 << 20),
        name="squeeze_and_first_shares",
    )(position, firsts, counts, table, received, u_block)


def next_shares(steps, position, u_block, tile):
    depth, cols = tile.shape
    rows = 2 * u_block.shape[1]
    smem = pl.BlockSpec(memory_space=pltpu.SMEM)
    vmem = pl.BlockSpec(memory_space=pltpu.VMEM)
    hbm = pl.BlockSpec(memory_space=pl.ANY)
    share = jax.ShapeDtypeStruct((len(steps), rows, cols // 2), F32)
    return pl.pallas_call(
        functools.partial(next_kernel, steps),
        in_specs=[smem, hbm, vmem],
        out_specs=(vmem, vmem),
        out_shape=(share, share),
        scratch_shapes=[
            pltpu.VMEM((len(steps), rows, depth), BF),
            pltpu.SemaphoreType.DMA((len(steps), 4)),
        ],
        cost_estimate=pl.CostEstimate(flops=12 << 30, bytes_accessed=16 << 20, transcendentals=0),
        compiler_params=pltpu.CompilerParams(vmem_limit_bytes=24 << 20),
        name="next_shares",
    )(position, u_block, tile)


def pairs(target):
    result = []
    for r in range(8):
        for c in range(16):
            z, core, y, x = target(r // 2, r % 2, c // 4, c % 4)
            result.append((r * 16 + c, (2 * z + core) * 16 + 4 * y + x))
    return result


def local(parent_cov, anc_index, fac_rows, inv_factor, own_inverse):
    row_count = lax.axis_size("row")
    col_count = lax.axis_size("col")
    owners = row_count * col_count
    parent_rows = parent_cov.shape[0]
    tile_cols = anc_index.shape[0] // col_count
    sep_cols = inv_factor.shape[1]
    row_index = lax.axis_index("row")
    col_index = lax.axis_index("col")
    core = row_index % 2
    device = jnp.reshape(row_index * col_count + col_index, (1,)).astype(I32)
    position = jnp.stack([row_index // 2, core]).astype(I32)
    both = ("row", "col")
    swap = pairs(lambda z, core, y, x: (z, 1 - core, y, x))

    own_ids = lax.dynamic_slice_in_dim(anc_index, col_index * tile_cols, tile_cols)
    rank = jnp.sum((own_ids[None, :] < own_ids[:, None]).astype(I32), axis=1)
    perm = (jnp.arange(tile_cols, dtype=I32)[:, None] == rank[None, :]).astype(BF)
    row_ids = jnp.arange(inv_factor.shape[0], dtype=I32)[:, None]
    col_ids = row_index * sep_cols + jnp.arange(sep_cols, dtype=I32)[None, :]
    lower = jnp.where(row_ids >= col_ids, inv_factor, jnp.zeros((), inv_factor.dtype))
    u_tile = jnp.dot(fac_rows, lower, preferred_element_type=F32).astype(BF)
    u_t = lax.dot_general(
        u_tile, perm, (((0,), (1,)), ((), ())), preferred_element_type=F32
    ).astype(BF)
    piece = lax.ppermute(
        u_t, both, pairs(lambda z, core, y, x: (y, x // 2, z, 2 * (x % 2) + core))
    )
    slots, table, firsts, counts = index_tables(anc_index, owners, parent_rows, col_count)
    data = sort_columns(parent_cov, slots, row_count)
    piece, data = lax.optimization_barrier((piece, data))
    u_block = lax.all_gather(piece, "col", axis=0)
    outgoing = pack_columns(data, slots, table, firsts, counts, device, tile_cols)
    u_cols = lax.all_gather(u_t, "row", axis=0, tiled=True)
    outgoing, u_cols = lax.optimization_barrier((outgoing, u_cols))
    flat_out = outgoing.reshape(owners * SLOT, tile_cols)
    received = lax.all_to_all(flat_out, both, split_axis=0, concat_axis=0, tiled=True)
    received = received.reshape(owners, SLOT, tile_cols)

    tile, keep, give = first_shares((2, 1), position, firsts, counts, table, received, u_block)
    first = (keep + lax.ppermute(give, both, swap)).astype(BF)
    keep, give = next_shares((3, 0), position, u_block, tile)
    second = keep + lax.ppermute(give, both, swap)
    total = second[1]
    for step, share in ((2, first[0]), (1, first[1]), (3, second[0].astype(BF))):
        share = lax.ppermute(
            share, both, pairs(lambda z, core, y, x, step=step: ((z + step) % 4, core, y, x))
        )
        total = total + share.astype(F32)
    total = -total
    kept = lax.dynamic_slice_in_dim(total, core * sep_cols, sep_cols, axis=0)
    given = lax.dynamic_slice_in_dim(total, (1 - core) * sep_cols, sep_cols, axis=0)
    taken = lax.ppermute(given, both, swap)
    sa_sorted = jnp.concatenate(
        [jnp.where(core == 0, kept, taken), jnp.where(core == 0, taken, kept)], axis=1
    )

    sa_high = sa_sorted.astype(BF)
    ss_part = dot_nt(u_cols, sa_high).astype(BF)
    ss_all = lax.all_to_all(ss_part, "col", split_axis=0, concat_axis=0, tiled=True)
    sa_low = (sa_sorted - sa_high.astype(F32)).astype(BF)
    cov_sa = dot(sa_high, perm) + dot(sa_low, perm)
    ss_sum = jnp.sum(ss_all.reshape(col_count, -1, ss_all.shape[1]).astype(F32), axis=0)
    cov_ss = own_inverse - ss_sum.T
    return (cov_sa, cov_ss)


def solution(mesh):
    return jax.shard_map(
        local,
        mesh=mesh,
        in_specs=(P(("row", "col"), None), P(), P("col", None), P(None, "row"), P("row", "col")),
        out_specs=(P("row", "col"), P("row", "col")),
        check_vma=False,
    )
```

```python
import functools

import jax
import jax.numpy as jnp
from jax import lax
from jax.experimental import pallas as pl
from jax.experimental.pallas import tpu as pltpu
from jax.sharding import PartitionSpec as P

BF = jnp.bfloat16
F32 = jnp.float32
I32 = jnp.int32
SLOT = 32
LANES = 128
REACH = 10
LINES = 32
WIN = 256

def dot_nt(a, b):
    return lax.dot_general(a, b, (((1,), (1,)), ((), ())), preferred_element_type=F32)


def dot(a, b):
    return jnp.dot(a, b, preferred_element_type=F32)


def iota(shape, axis):
    return lax.broadcasted_iota(I32, shape, axis)


def ones_where(cond):
    return jnp.where(cond, 1.0, 0.0).astype(BF)


def index_kernel(tiles, anc_ref, slots_ref, table_ref, first_ref, count_ref):
    owners, rows = slots_ref.shape
    chunk = anc_ref.shape[1]
    tile_of = jnp.zeros((owners, rows), F32)
    for j in range(anc_ref.shape[0]):
        ids = anc_ref[j:j + 1, :]
        owner, inner = ids // rows, ids % rows
        tile = ((iota((1, chunk), 1) + j * chunk) // (anc_ref.shape[0] * chunk // tiles) + 1).astype(F32)
        owner_hot = jnp.where(iota((owners, chunk), 0) == owner, tile, 0.0).astype(BF)
        inner_hot = ones_where(iota((rows, chunk), 0) == inner)
        tile_of = tile_of + dot_nt(owner_hot, inner_hot)
    at = iota((rows, rows + LANES), 1)
    before = ones_where((iota((rows, rows + LANES), 0) < at) | (at >= rows))
    below = ones_where(iota((owners, owners), 1) < iota((owners, owners), 0))
    per_line = LANES // SLOT
    lines = owners // per_line
    pick = ones_where(iota((lines, owners), 1) // per_line == iota((lines, owners), 0))
    spread = iota((owners, LANES), 0) % per_line == iota((owners, LANES), 1) // SLOT
    s = (iota((lines, LANES), 1) % SLOT).astype(F32)
    edge = (iota((owners, LANES), 1) * WIN).astype(F32)
    expand = lambda v: dot(pick, jnp.where(spread, v, 0.0).astype(BF))
    slots = jnp.zeros((owners, rows), F32) - 1.0
    tile_len = float(anc_ref.shape[0] * chunk // tiles)
    prev = None
    for c in range(tiles):
        mask = tile_of == float(c + 1)
        both = dot(ones_where(mask), before)
        ahead, number = both[:, :rows], both[:, rows:]
        start = dot(below, number.astype(BF))
        base = float(c // 2 * SLOT + 1)
        lift = ahead + base
        if c % 2:
            lift = lift + jnp.concatenate([prev[0]] * (rows // LANES), axis=1)
        slots = slots + jnp.where(mask, lift, 0.0)
        high = jnp.floor(start * (1.0 / 32.0))
        n = expand(number)
        p = expand(high) * 32.0 + expand(start - high * 32.0)
        end = start + number
        lead = jnp.sum(jnp.where(end <= edge, 1.0, 0.0), axis=0, keepdims=True).astype(I32)
        last = jnp.sum(jnp.where(start < edge + float(WIN), 1.0, 0.0), axis=0, keepdims=True).astype(I32) - 1
        first = lead // per_line
        first_ref[c:c + 1, :] = first
        count_ref[c:c + 1, :] = (last // per_line - first) // REACH + 1
        if c % 2:
            n0, p0 = prev[1], prev[2]
            to = jnp.where(s < n0, p0 + s, jnp.where(s < n0 + n, tile_len + p + s - n0, -1.0))
            table_ref[c // 2, 0:lines, :] = to.astype(I32)
        prev = (number, n, p)
    slots_ref[...] = slots.astype(I32)


def index_tables(anc, owners, rows, tiles):
    lines = owners * SLOT // LANES
    return pl.pallas_call(
        functools.partial(index_kernel, tiles),
        out_shape=(
            jax.ShapeDtypeStruct((owners, rows), I32),
            jax.ShapeDtypeStruct((tiles // 2, lines, LANES), I32),
            jax.ShapeDtypeStruct((tiles, LANES), I32),
            jax.ShapeDtypeStruct((tiles, LANES), I32),
        ),
        cost_estimate=pl.CostEstimate(flops=8 << 30, bytes_accessed=1 << 20, transcendentals=0),
        name="index_tables",
    )(anc.reshape(-1, 2048))


def one_hot(targets, base):
    ids = iota((WIN, targets.shape[-1]), 0) + base
    return ones_where(ids == targets)


def window_hot(table, lead, first, base):
    start = jnp.minimum(first, LINES - REACH)
    lines = []
    for i in range(REACH):
        line = table[lead + (pl.ds(start + i, 1), slice(None))]
        lines.append(one_hot(jnp.where(start + i < first, -1, line), base))
    return start, jnp.concatenate(lines, axis=1)


def sort_kernel(per_step, slots_ref, cov_ref, out_ref):
    cols = slots_ref.shape[-1]
    for k in range(per_step):
        hot = one_hot(slots_ref[pl.ds(pl.program_id(0) * per_step + k, 1), :], 0)
        part = dot_nt(hot, cov_ref[:, k * cols:(k + 1) * cols]).astype(BF)
        for b in range(out_ref.shape[0]):
            out_ref[b, k * SLOT:(k + 1) * SLOT, :] = part[b * SLOT:(b + 1) * SLOT]


def sort_columns(cov, slots, blocks, per_step=32):
    rows, width = cov.shape
    ranges, cols = slots.shape
    return pl.pallas_call(
        functools.partial(sort_kernel, per_step),
        grid=(ranges // per_step,),
        in_specs=[
            pl.BlockSpec(slots.shape, lambda i: (0, 0)),
            pl.BlockSpec((rows, per_step * cols), lambda i: (0, i)),
        ],
        out_specs=pl.BlockSpec((blocks, per_step * SLOT, rows), lambda i: (0, i, 0)),
        out_shape=jax.ShapeDtypeStruct((blocks, ranges * SLOT, rows), BF),
        cost_estimate=pl.CostEstimate(flops=12 << 30, bytes_accessed=32 << 20, transcendentals=0),
        name="sort_columns",
    )(slots, cov)


def pack_kernel(first_ref, count_ref, dev_ref, slots_ref, table_ref, data_ref, out_ref, acc):
    block = pl.program_id(0)
    blocks, group, _, width = out_ref.shape
    windows = width // WIN
    rows_hot = one_hot(slots_ref[pl.ds(dev_ref[0], 1), :], 0)

    def part(first, base):
        start, hot = window_hot(table_ref, (block,), first, base)
        at = pl.multiple_of(start * LANES, LANES)
        return dot(hot, data_ref[0, pl.ds(at, REACH * LANES), :]).astype(BF)

    for job in range(group * windows):
        tile = block * group + job // windows
        acc[job * WIN:(job + 1) * WIN, :] = part(first_ref[tile, job % windows], job * WIN)

    def extra(job, carry):
        tile, w = block * group + job // windows, lax.rem(job, windows)
        at = pl.multiple_of(job * WIN, WIN)

        def more(i, carry):
            acc[pl.ds(at, WIN), :] += part(first_ref[tile, w] + i * REACH, at)
            return carry

        return lax.fori_loop(1, count_ref[tile, w], more, carry)

    most = count_ref[block * group, 0]
    for job in range(1, group * windows):
        most = jnp.maximum(most, count_ref[block * group + job // windows, job % windows])

    @pl.when(most > 1)
    def _():
        lax.fori_loop(0, group * windows, extra, 0)

    for g in range(group):
        out = dot_nt(rows_hot, acc[g * width:(g + 1) * width, :]).astype(BF)
        for b in range(blocks):
            out_ref[b, g] = out[b * SLOT:(b + 1) * SLOT]


def pack_columns(data, slots, table, firsts, counts, device, tile_cols):
    blocks, length, rows = data.shape
    tiles = firsts.shape[0]
    group = tiles // blocks
    grid_spec = pltpu.PrefetchScalarGridSpec(
        num_scalar_prefetch=3,
        grid=(blocks,),
        in_specs=[
            pl.BlockSpec(slots.shape, lambda i, f, n, d: (0, 0)),
            pl.BlockSpec(table.shape, lambda i, f, n, d: (0, 0, 0)),
            pl.BlockSpec((1, length, rows), lambda i, f, n, d: (i, 0, 0)),
        ],
        out_specs=pl.BlockSpec((blocks, group, SLOT, tile_cols), lambda i, f, n, d: (0, i, 0, 0)),
        scratch_shapes=[pltpu.VMEM((group * tile_cols, rows), BF)],
    )
    return pl.pallas_call(
        pack_kernel,
        grid_spec=grid_spec,
        out_shape=jax.ShapeDtypeStruct((blocks, tiles, SLOT, tile_cols), BF),
        cost_estimate=pl.CostEstimate(flops=12 << 30, bytes_accessed=24 << 20, transcendentals=0),
        name="pack_columns",
    )(firsts, counts, device, slots, table, data)


def load_lhs(z, u_ref, lhs, sems):
    rows, cols = u_ref.shape[1:]
    return [
        pltpu.make_async_copy(
            u_ref.at[4 * z + 2 * half + core],
            lhs.at[pl.ds(core * rows, rows), pl.ds(half * cols, cols)],
            sems.at[2 * half + core],
        )
        for half in range(2) for core in range(2)
    ]


def start_loads(steps, pos_ref, u_ref, lhs, sems):
    jobs = []
    for n, step in enumerate(steps):
        jobs.append(load_lhs(lax.rem(pos_ref[0] + step, 4), u_ref, lhs.at[n], sems.at[n]))
        for copy in jobs[n]:
            copy.start()
    return jobs


def multiply(jobs, lhs, tile_ref, core, keep_ref, give_ref):
    half = keep_ref.shape[2]
    give = pl.multiple_of((1 - core) * half, half)
    keep = pl.multiple_of(core * half, half)
    for n, copies in enumerate(jobs):
        for copy in copies:
            copy.wait()
        give_ref[n] = dot(lhs[n], tile_ref[:, pl.ds(give, half)]).astype(BF)
        keep_ref[n] = dot(lhs[n], tile_ref[:, pl.ds(keep, half)])


def first_kernel(steps, pos_ref, first_ref, count_ref, table_ref, got_ref, u_ref,
                 tile_ref, keep_ref, give_ref, held, lhs, got_sem, lhs_sems):
    z, core = pos_ref[0], pos_ref[1]
    load = pltpu.make_async_copy(got_ref, held, got_sem)
    load.start()
    jobs = start_loads(steps, pos_ref, u_ref, lhs, lhs_sems)
    per_line = LANES // SLOT
    span = REACH * per_line
    windows = tile_ref.shape[0] // WIN
    block = 2 * z + core

    def part(first, base):
        start, hot = window_hot(table_ref, (block,), first, base)
        data = held[pl.ds(start * per_line, span)].reshape(REACH * LANES, held.shape[-1])
        return dot(hot, data).astype(BF)

    load.wait()
    for w in range(windows):
        tile, v = 2 * block + w // (windows // 2), w % (windows // 2)
        tile_ref[w * WIN:(w + 1) * WIN, :] = part(first_ref[tile, v], w * WIN)

    def window(w, carry):
        tile, v = 2 * block + w // (windows // 2), lax.rem(w, windows // 2)
        at = pl.multiple_of(w * WIN, WIN)

        def more(i, carry):
            tile_ref[pl.ds(at, WIN), :] += part(first_ref[tile, v] + i * REACH, at)
            return carry

        return lax.fori_loop(1, count_ref[tile, v], more, carry)

    lax.fori_loop(0, windows, window, 0)
    multiply(jobs, lhs, tile_ref, core, keep_ref, give_ref)


def next_kernel(steps, pos_ref, u_ref, tile_ref, keep_ref, give_ref, lhs, sems):
    jobs = start_loads(steps, pos_ref, u_ref, lhs, sems)
    multiply(jobs, lhs, tile_ref, pos_ref[1], keep_ref, give_ref)


def first_shares(steps, position, firsts, counts, table, received, u_block):
    owners, _, cols = received.shape
    rows, depth = 2 * u_block.shape[1], 2 * u_block.shape[2]
    smem = pl.BlockSpec(memory_space=pltpu.SMEM)
    vmem = pl.BlockSpec(memory_space=pltpu.VMEM)
    hbm = pl.BlockSpec(memory_space=pl.ANY)
    share = jax.ShapeDtypeStruct((len(steps), rows, cols // 2), F32)
    return pl.pallas_call(
        functools.partial(first_kernel, steps),
        in_specs=[smem, smem, smem, vmem, hbm, hbm],
        out_specs=(vmem, vmem, vmem),
        out_shape=(pltpu.VMEM((depth, cols), BF), share, jax.ShapeDtypeStruct(share.shape, BF)),
        scratch_shapes=[
            pltpu.VMEM((owners, SLOT, cols), BF),
            pltpu.VMEM((len(steps), rows, depth), BF),
            pltpu.SemaphoreType.DMA,
            pltpu.SemaphoreType.DMA((len(steps), 4)),
        ],
        cost_estimate=pl.CostEstimate(flops=24 << 30, bytes_accessed=24 << 20, transcendentals=0),
        compiler_params=pltpu.CompilerParams(vmem_limit_bytes=36 << 20),
        name="squeeze_and_first_shares",
    )(position, firsts, counts, table, received, u_block)


def next_shares(steps, position, u_block, tile):
    depth, cols = tile.shape
    rows = 2 * u_block.shape[1]
    smem = pl.BlockSpec(memory_space=pltpu.SMEM)
    vmem = pl.BlockSpec(memory_space=pltpu.VMEM)
    hbm = pl.BlockSpec(memory_space=pl.ANY)
    share = jax.ShapeDtypeStruct((len(steps), rows, cols // 2), F32)
    return pl.pallas_call(
        functools.partial(next_kernel, steps),
        in_specs=[smem, hbm, vmem],
        out_specs=(vmem, vmem),
        out_shape=(share, jax.ShapeDtypeStruct(share.shape, BF)),
        scratch_shapes=[
            pltpu.VMEM((len(steps), rows, depth), BF),
            pltpu.SemaphoreType.DMA((len(steps), 4)),
        ],
        cost_estimate=pl.CostEstimate(flops=12 << 30, bytes_accessed=16 << 20, transcendentals=0),
        compiler_params=pltpu.CompilerParams(vmem_limit_bytes=24 << 20),
        name="next_shares",
    )(position, u_block, tile)


def pairs(target):
    result = []
    for r in range(8):
        for c in range(16):
            z, core, y, x = target(r // 2, r % 2, c // 4, c % 4)
            result.append((r * 16 + c, (2 * z + core) * 16 + 4 * y + x))
    return result


def local(parent_cov, anc_index, fac_rows, inv_factor, own_inverse):
    row_count = lax.axis_size("row")
    col_count = lax.axis_size("col")
    owners = row_count * col_count
    parent_rows = parent_cov.shape[0]
    tile_cols = anc_index.shape[0] // col_count
    sep_cols = inv_factor.shape[1]
    row_index = lax.axis_index("row")
    col_index = lax.axis_index("col")
    core = row_index % 2
    device = jnp.reshape(row_index * col_count + col_index, (1,)).astype(I32)
    position = jnp.stack([row_index // 2, core]).astype(I32)
    both = ("row", "col")
    swap = pairs(lambda z, core, y, x: (z, 1 - core, y, x))

    own_ids = lax.dynamic_slice_in_dim(anc_index, col_index * tile_cols, tile_cols)
    rank = jnp.sum((own_ids[None, :] < own_ids[:, None]).astype(I32), axis=1)
    perm = (jnp.arange(tile_cols, dtype=I32)[:, None] == rank[None, :]).astype(BF)
    row_ids = jnp.arange(inv_factor.shape[0], dtype=I32)[:, None]
    col_ids = row_index * sep_cols + jnp.arange(sep_cols, dtype=I32)[None, :]
    lower = jnp.where(row_ids >= col_ids, inv_factor, jnp.zeros((), inv_factor.dtype))
    u_tile = jnp.dot(fac_rows, lower, preferred_element_type=F32).astype(BF)
    u_t = lax.dot_general(
        u_tile, perm, (((0,), (1,)), ((), ())), preferred_element_type=F32
    ).astype(BF)
    piece = lax.ppermute(
        u_t, both, pairs(lambda z, core, y, x: (y, x // 2, z, 2 * (x % 2) + core))
    )
    slots, table, firsts, counts = index_tables(anc_index, owners, parent_rows, col_count)
    data = sort_columns(parent_cov, slots, row_count)
    piece, data = lax.optimization_barrier((piece, data))
    u_block = lax.all_gather(piece, "col", axis=0)
    outgoing = pack_columns(data, slots, table, firsts, counts, device, tile_cols)
    outgoing, u_t = lax.optimization_barrier((outgoing, u_t))
    u_cols = lax.all_gather(u_t, "row", axis=0, tiled=True)
    flat_out = outgoing.reshape(owners * SLOT, tile_cols)
    received = lax.all_to_all(flat_out, both, split_axis=0, concat_axis=0, tiled=True)
    received = received.reshape(owners, SLOT, tile_cols)

    tile, keep, give = first_shares((2, 1), position, firsts, counts, table, received, u_block)
    first = (keep + lax.ppermute(give, both, swap).astype(F32)).astype(BF)
    keep, give = next_shares((3, 0), position, u_block, tile)
    second = keep + lax.ppermute(give, both, swap).astype(F32)
    total = second[1]
    for step, share in ((2, first[0]), (1, first[1]), (3, second[0].astype(BF))):
        share = lax.ppermute(
            share, both, pairs(lambda z, core, y, x, step=step: ((z + step) % 4, core, y, x))
        )
        total = total + share.astype(F32)
    total = -total
    kept = lax.dynamic_slice_in_dim(total, core * sep_cols, sep_cols, axis=0)
    given = lax.dynamic_slice_in_dim(total, (1 - core) * sep_cols, sep_cols, axis=0)
    taken = lax.ppermute(given, both, swap)
    sa_sorted = jnp.concatenate(
        [jnp.where(core == 0, kept, taken), jnp.where(core == 0, taken, kept)], axis=1
    )

    sa_high = sa_sorted.astype(BF)
    ss_part = dot_nt(u_cols, sa_high).astype(BF)
    ss_all = lax.all_to_all(ss_part, "col", split_axis=0, concat_axis=0, tiled=True)
    sa_low = (sa_sorted - sa_high.astype(F32)).astype(BF)
    cov_sa = dot(sa_high, perm) + dot(sa_low, perm)
    ss_sum = jnp.sum(ss_all.reshape(col_count, -1, ss_all.shape[1]).astype(F32), axis=0)
    cov_ss = own_inverse - ss_sum.T
    return (cov_sa, cov_ss)


def solution(mesh):
    return jax.shard_map(
        local,
        mesh=mesh,
        in_specs=(P(("row", "col"), None), P(), P("col", None), P(None, "row"), P("row", "col")),
        out_specs=(P("row", "col"), P("row", "col")),
        check_vma=False,
    )
```
